32 devices in a mesh: groups: 2 (over y), space: 8 (over z, x), section: 2 (over core).
Axes of the slice: x: 2, y: 2, z: 4, core: 2. Of those that a mesh axis runs over, the one named last changes fastest.
Arguments:
- atm_state: bfloat16 [4, 8, 256, 256], P(('groups', 'section'), 'space'), parts along dimension 0, may hold values from -6 to 6
- ocean_state: bfloat16 [4, 2048, 192], P(('groups', 'section'), 'space'), parts along dimension 0, may hold values from -6 to 6
- owners: int32 [8, 256, 2], P('space'), may hold values from 0 to 7, all different within a row; in each aligned block of 256 rows (0 to 255, 256 to 511, ..., all dimensions but the last counted through in order) at most 128 rows name the same one
- target_cell: int32 [8, 256, 2], P('space'), may hold values from 0 to 255
- margin_weight: float32 [8, 256, 2], P('space'), may hold values from 0.25 to 1
- sea_mask: int32 [8, 256], P('space'), may hold values 0 or 1
- conv_kernel: bfloat16 [9, 256, 256], replicated, may hold values from -0.125 to 0.125
- meridional_weight: bfloat16 [256, 256], replicated, may hold values from -0.375 to 0.375
- atm_gain: float32 [256], replicated, may hold values from 0.25 to 1.75
- atm_in: bfloat16 [256, 1024], replicated, may hold values from -0.375 to 0.375
- atm_out: bfloat16 [1024, 256], replicated, may hold values from -0.1875 to 0.1875
- flux_weight: bfloat16 [256, 128], replicated, may hold values from -0.375 to 0.375
- forcing_weight: bfloat16 [128, 192], replicated, may hold values from -0.5 to 0.5
- ocean_gain: float32 [192], replicated, may hold values from 0.25 to 1.75
- ocean_in: bfloat16 [192, 768], replicated, may hold values from -0.4375 to 0.4375
- ocean_out: bfloat16 [768, 192], replicated, may hold values from -0.21875 to 0.21875
- surface_weight: bfloat16 [192, 128], replicated, may hold values from -0.4375 to 0.4375
- feedback_weight: bfloat16 [128, 256], replicated, may hold values from -0.5 to 0.5
Outputs:
- atm_next: bfloat16 [4, 8, 256, 256], P(('groups', 'section'), 'space'), parts along dimension 0
- ocean_next: bfloat16 [4, 2048, 192], P(('groups', 'section'), 'space'), parts along dimension 0
The draws below stay inside these ranges and needn't reach their ends.
There are 2 independent parts, one for each index of `groups`. The reference program is written for one: setup_inputs(seed, part) draws one part's arguments, and reference() takes and returns one part's arrays. A program takes and returns all parts, laid end to end along the dimension named above; an argument that names none is the same for every part. Nothing has to cross between parts.
Inputs may be any that keep to these rules, and one draw needn't show every extreme that they name: Within the 256 cells of one latitude band, no owner is named by more than 128 margin entries, a bound that some block reaches; the 2 owners of one cell differ.
All inputs are finite; a program needn't handle non-finite values. No bound on the sum of `sea_mask` on one device may be relied on, other than what follows from the above.
Results may differ from the reference program's by a relative error of at most 0.014.
Values may be sent and summed in bfloat16 or wider, within the bound.
A program may use at most 64 MiB of HBM per device.

```python
import math
import jax
import jax.numpy as jnp
import numpy as np
from jax import lax

LAT_DEV = 1
LON = 256
ATM_CH = 256
ATM_HID = 1024
OCN_CH = 192
OCN_HID = 768
FLUX_CH = 128
MARGINS = 2
MEMBERS = 2
NLAT = 8
OCN_DEV = 256
OCN_CELLS = 2048
SLOTS = 128
N_SPACE = 8


def set_ends(array, key, least, high):
    spot = [jax.random.randint(jax.random.fold_in(key, axis), (), 0, length) for axis, length in enumerate(array.shape)]
    main_axis = array.shape.index(max(array.shape))
    beside = spot[:main_axis] + [(spot[main_axis] + 1) % array.shape[main_axis]] + spot[main_axis + 1:]
    return array.at[tuple(spot)].set(least).at[tuple(beside)].set(high)


def steps_of(own_key, dims, split, smallest, high):
    level = 1.0
    for dim, shards_of in split:
        draws = jax.random.uniform(jax.random.fold_in(jax.random.fold_in(own_key, 6), dim), (shards_of,), jnp.float32, smallest / len(split), high / len(split))
        level = level * jnp.repeat(jnp.exp(draws), dims[dim] // shards_of).reshape((-1,) + (1,) * (len(dims) - 1 - dim))
    return level


def deal_out(stream_key, own, number, rows, count, top, most, lean):
    sequence = jax.random.permutation(stream_key, count)
    packed, usual = portions_of(count, rows * top, most, lean, True), portions_of(count, rows * top, most, lean, False)
    places = jnp.arange(count)

    def named(lengths, rotation):
        used = int((lengths > 0).sum())
        fixed = max(1, used // 4)
        passed = fixed + (places - fixed + rotation * (used - fixed)) % max(1, count - fixed)
        return jnp.zeros((count,), jnp.int32).at[sequence[jnp.where(places < fixed, places, passed)]].set(jnp.asarray(lengths, jnp.int32))

    lengths = jnp.where(number % 4 == 0, named(packed, number // 4), named(usual, number - number // 4 - 1))
    mixed = jax.random.permutation(jax.random.fold_in(own, 3), count)
    donor, taker = mixed[0:count // 2 * 2:2], mixed[1:count // 2 * 2:2]
    slack = jnp.minimum(lengths[donor] - 1, most - lengths[taker]) // 2
    slack = jnp.where((donor == sequence[0]) | (taker == sequence[0]) | (lengths[taker] == 0), 0, jnp.maximum(slack, 0))
    passed = jax.random.randint(jax.random.fold_in(own, 4), (count // 2,), 0, 1 << 20) % (slack + 1)
    lengths = lengths.at[donor].add(-passed).at[taker].add(passed)
    items = jnp.searchsorted(jnp.cumsum(lengths), jnp.arange(rows * top), side="right").astype(jnp.int32)
    listing = items.reshape(top, rows).T
    listing = listing[jax.random.permutation(jax.random.fold_in(own, 1), rows)]
    rotation = jax.random.randint(jax.random.fold_in(own, 2), (rows, 1), 0, top)
    return jnp.take_along_axis(listing, (jnp.arange(top)[None, :] + rotation) % top, axis=1)


def portions_of(number_of, total, reach, skew, full):
    loads = [(1 << 20) // math.isqrt(rank ** skew) + 1 for rank in range(1, number_of + 1)]
    largest = reach if full else min(reach, max(-(-total // number_of), total * loads[0] // sum(loads)))
    least = 1 if total - largest >= number_of - 1 else 0
    counts, spare = [largest] + [least] * (number_of - 1), total - largest - least * (number_of - 1)
    while spare > 0:
        candidates = [i for i in range(1, number_of) if counts[i] < largest] or [i for i in range(1, number_of) if counts[i] < reach]
        pool, left = sum([loads[i] for i in candidates]), spare
        for i in candidates:
            addition = min(reach - counts[i], max(1, left * loads[i] // pool), spare)
            counts[i] = counts[i] + addition
            spare = spare - addition
    return np.array(counts)


def gaussian(own_key, extent, spread, bound, cuts=(), dtype=jnp.bfloat16):
    loudness = steps_of(own_key, extent, cuts, -0.22, 0.18) if cuts else 1.0
    entries = jax.random.normal(own_key, extent, jnp.float32) * spread * loudness
    return jnp.minimum(jnp.maximum(entries, -bound), bound).astype(dtype)


def setup_inputs(seed: int = 0, part: int = 0) -> dict:
    arg_keys = jax.random.split(jax.random.key(seed), 19)
    own_keys = jax.random.split(jax.random.fold_in(arg_keys[18], part), 19)
    atm_state = gaussian(own_keys[0], (MEMBERS, NLAT, LON, ATM_CH), 1.0, 6.0, ((0, 2), (1, 8)))
    ocean_state = gaussian(own_keys[1], (MEMBERS, OCN_CELLS, OCN_CH), 1.0, 6.0, ((0, 2), (1, 8)))
    owners_keys = jax.random.split(jax.random.fold_in(arg_keys[2], 1), NLAT * LON // (LAT_DEV * LON))
    owners_turns = jax.random.permutation(jax.random.fold_in(arg_keys[2], 3), NLAT * LON // (LAT_DEV * LON))
    owners = jax.vmap(lambda own, number: deal_out(jax.random.fold_in(arg_keys[2], 2), own, number, LAT_DEV * LON, N_SPACE, MARGINS, SLOTS, 2))(owners_keys, owners_turns).reshape((NLAT, LON, MARGINS))
    target_cell = set_ends(jax.random.randint(arg_keys[3], (NLAT, LON, MARGINS), 0, OCN_DEV), jax.random.fold_in(arg_keys[3], 1), 0, OCN_DEV - 1).astype(jnp.int32)
    margin_weight = jnp.clip(0.25 + 0.75 * jax.random.uniform(arg_keys[4], (NLAT, LON, MARGINS), jnp.float32) ** steps_of(arg_keys[4], (NLAT, LON, MARGINS), ((0, 8),), -0.2, 0.2), 0.25, 1.0)
    sea_mask = set_ends((jax.random.randint(arg_keys[5], (NLAT, LON), 0, 10) < 7).astype(jnp.int32), jax.random.fold_in(arg_keys[5], 1), 0, 1)
    conv_kernel = gaussian(arg_keys[6], (9, ATM_CH, ATM_CH), (9 * ATM_CH) ** -0.5, 0.125)
    meridional_weight = gaussian(arg_keys[7], (ATM_CH, ATM_CH), ATM_CH ** -0.5, 0.375)
    atm_gain = jnp.clip(1.0 + 0.15 * jax.random.normal(arg_keys[8], (ATM_CH,), jnp.float32), 0.25, 1.75)
    atm_in = gaussian(arg_keys[9], (ATM_CH, ATM_HID), ATM_CH ** -0.5, 0.375)
    atm_out = gaussian(arg_keys[10], (ATM_HID, ATM_CH), ATM_HID ** -0.5, 0.1875)
    flux_weight = gaussian(arg_keys[11], (ATM_CH, FLUX_CH), ATM_CH ** -0.5, 0.375)
    forcing_weight = gaussian(arg_keys[12], (FLUX_CH, OCN_CH), FLUX_CH ** -0.5, 0.5)
    ocean_gain = jnp.clip(1.0 + 0.15 * jax.random.normal(arg_keys[13], (OCN_CH,), jnp.float32), 0.25, 1.75)
    ocean_in = gaussian(arg_keys[14], (OCN_CH, OCN_HID), OCN_CH ** -0.5, 0.4375)
    ocean_out = gaussian(arg_keys[15], (OCN_HID, OCN_CH), OCN_HID ** -0.5, 0.21875)
    surface_weight = gaussian(arg_keys[16], (OCN_CH, FLUX_CH), OCN_CH ** -0.5, 0.4375)
    feedback_weight = gaussian(arg_keys[17], (FLUX_CH, ATM_CH), FLUX_CH ** -0.5, 0.5)
    return {"atm_state": atm_state, "ocean_state": ocean_state, "owners": owners, "target_cell": target_cell, "margin_weight": margin_weight, "sea_mask": sea_mask, "conv_kernel": conv_kernel, "meridional_weight": meridional_weight, "atm_gain": atm_gain, "atm_in": atm_in, "atm_out": atm_out, "flux_weight": flux_weight, "forcing_weight": forcing_weight, "ocean_gain": ocean_gain, "ocean_in": ocean_in, "ocean_out": ocean_out, "surface_weight": surface_weight, "feedback_weight": feedback_weight}


def conv_taps(padded, kernel, lat_rows):
    channels = padded.shape[-1]
    columns = []
    for row_off in range(3):
        lat_band = padded[row_off:row_off + lat_rows]
        for col_off in range(3):
            columns.append(jnp.roll(lat_band, 1 - col_off, axis=1))
    stacked = jnp.concatenate(columns, axis=-1)
    flattened = stacked.reshape(-1, 9 * channels)
    result = jnp.dot(flattened, kernel.reshape(9 * channels, channels), preferred_element_type=jnp.float32)
    return result.reshape(lat_rows, padded.shape[1], channels)

def rms_scale(values, gain_vec):
    return values * lax.rsqrt(lax.optimization_barrier(jnp.mean(values * values, axis=-1, keepdims=True)) + 1e-06) * gain_vec

def reference(atm_state, ocean_state, owners, target_cell, margin_weight, sea_mask, conv_kernel, meridional_weight, atm_gain, atm_in, atm_out, flux_weight, forcing_weight, ocean_gain, ocean_in, ocean_out, surface_weight, feedback_weight):
    sea_cells = sea_mask.astype(jnp.float32).reshape(-1)
    weights = margin_weight.reshape(-1, MARGINS)
    target = (owners * OCN_DEV + target_cell).reshape(-1).astype(jnp.int32)

    def member(states):
        atm_one, ocn_one = states
        padded = jnp.pad(atm_one, ((1, 1), (0, 0), (0, 0)))
        mixing = conv_taps(padded, conv_kernel, NLAT)
        hidden = atm_one.astype(jnp.float32) + mixing
        zonal_sums = lax.optimization_barrier(jnp.sum(hidden, axis=1)) / math.sqrt(LON)
        prefix = (jnp.cumsum(zonal_sums, axis=0) - zonal_sums) / math.sqrt(NLAT)
        meridional = jnp.dot(prefix, meridional_weight.astype(jnp.float32), precision=lax.Precision.HIGHEST)
        lifted = (hidden + meridional[:, None, :]).reshape(-1, ATM_CH)
        normed = rms_scale(lifted, atm_gain).astype(jnp.bfloat16)
        activated = jax.nn.silu(jnp.dot(normed, atm_in, preferred_element_type=jnp.float32)).astype(jnp.bfloat16)
        atm_mid = (lifted + jnp.dot(activated, atm_out, preferred_element_type=jnp.float32)).astype(jnp.bfloat16)
        flux_rows = jnp.dot(atm_mid, flux_weight, preferred_element_type=jnp.float32)
        payload = (weights[:, :, None] * sea_cells[:, None, None] * flux_rows[:, None, :]).astype(jnp.bfloat16)
        payload = payload.reshape(-1, FLUX_CH)
        forcing = jnp.zeros((OCN_CELLS, FLUX_CH), jnp.float32).at[target].add(payload.astype(jnp.float32))
        forcing = forcing.astype(jnp.bfloat16)
        ocean_lift = ocn_one.astype(jnp.float32) + jnp.dot(forcing, forcing_weight, preferred_element_type=jnp.float32)
        ocean_normed = rms_scale(ocean_lift, ocean_gain).astype(jnp.bfloat16)
        ocean_act = jax.nn.silu(jnp.dot(ocean_normed, ocean_in, preferred_element_type=jnp.float32)).astype(jnp.bfloat16)
        ocean_new = (ocean_lift + jnp.dot(ocean_act, ocean_out, preferred_element_type=jnp.float32)).astype(jnp.bfloat16)
        surface = jnp.dot(ocean_new, surface_weight, preferred_element_type=jnp.float32).astype(jnp.bfloat16)
        picked = surface[target].reshape(-1, MARGINS, FLUX_CH)
        feedback = lax.optimization_barrier(jnp.sum(weights[:, :, None] * picked.astype(jnp.float32), axis=1)).astype(jnp.bfloat16)
        back_term = jnp.dot(feedback, feedback_weight, preferred_element_type=jnp.float32)
        atm_new = (atm_mid.astype(jnp.float32) + sea_cells[:, None] * back_term).astype(jnp.bfloat16)
        return (atm_new.reshape(NLAT, LON, ATM_CH), ocean_new)
    atm_next, ocean_next = lax.map(member, (atm_state, ocean_state))
    return (atm_next, ocean_next)
```

```python
import functools
import math

import jax
import jax.numpy as jnp
from jax import lax
from jax.experimental import pallas as pl
from jax.experimental.pallas import tpu as pltpu
from jax.sharding import PartitionSpec as P

F32 = jnp.float32
BF16 = jnp.bfloat16


def mm(left, right):
    return jnp.dot(left, right, preferred_element_type=F32)


def mm_nt(left, right):
    return lax.dot_general(left, right, (((1,), (1,)), ((), ())), preferred_element_type=F32)


def rms_scale(values, gain_vec):
    return values * lax.rsqrt(jnp.mean(values * values, axis=-1, keepdims=True) + 1e-06) * gain_vec


def silu(values):
    return values / (1.0 + jnp.exp(-values))


def thirds(rows):
    high = rows.astype(BF16).astype(F32)
    rest = rows - high
    middle = rest.astype(BF16).astype(F32)
    low = rest - middle
    row = lax.broadcasted_iota(jnp.int32, rows.shape, 0)
    return jnp.where(
        row == 0, high, jnp.where(row == 1, middle, jnp.where(row == 2, low, 0.0))
    ).astype(BF16)


def each(count, body):
    if count <= 8:
        for step in range(count):
            body(step)
    else:
        lax.fori_loop(0, count, lambda step, carry: (body(step), carry)[1], 0)


def kernel(
    n,
    slots,
    atm_ref,
    own_ref,
    tgt_ref,
    wgt_ref,
    sea_ref,
    again_ref,
    ogain_ref,
    ocn_hbm,
    conv_hbm,
    mer_hbm,
    ain_hbm,
    aout_hbm,
    flux_hbm,
    forc_hbm,
    oin_hbm,
    oout_hbm,
    surf_hbm,
    feed_hbm,
    atm_out_ref,
    ocn_out_ref,
    ocn_v,
    conv_v,
    mer_v,
    ain_v,
    aout_v,
    flux_v,
    forc_v,
    oin_v,
    oout_v,
    surf_v,
    feed_v,
    north,
    south,
    sums_send,
    sums_all,
    cells_send,
    cells_all,
    pack,
    unpack,
    gather_t,
    gather,
    send_rows,
    recv_rows,
    back_rows,
    ret_rows,
    mid_v,
    ocn_new,
    load_sem,
    out_sem,
    halo_send,
    halo_recv,
    sum_send_sem,
    sum_recv_sem,
    cell_send_sem,
    cell_recv_sem,
    flux_send_sem,
    flux_recv_sem,
    back_send_sem,
    back_recv_sem,
):
    me = lax.axis_index("space")
    lon, channels = atm_ref.shape
    barrier = pltpu.get_barrier_semaphore()
    for d in range(1, n):
        pl.semaphore_signal(
            barrier,
            inc=1,
            device_id={"space": lax.rem(me + d, n)},
            device_id_type=pl.DeviceIdType.MESH,
        )

    loads = [
        pltpu.make_async_copy(src, dst, load_sem.at[i])
        for i, (src, dst) in enumerate(
            [
                (conv_hbm, conv_v),
                (mer_hbm, mer_v),
                (ain_hbm, ain_v),
                (aout_hbm, aout_v),
                (flux_hbm, flux_v),
                (ocn_hbm, ocn_v),
                (forc_hbm, forc_v),
                (oin_hbm, oin_v),
                (oout_hbm, oout_v),
                (surf_hbm, surf_v),
                (feed_hbm, feed_v),
            ]
        )
    ]
    for load in loads:
        load.start()

    def remote(src, dst, send_sem, recv_sem, peer):
        return pltpu.make_async_remote_copy(
            src_ref=src,
            dst_ref=dst,
            send_sem=send_sem,
            recv_sem=recv_sem,
            device_id={"space": peer},
            device_id_type=pl.DeviceIdType.MESH,
        )

    total = jnp.sum(atm_ref[...].astype(F32), axis=0, keepdims=True)
    sums_send[...] = jnp.broadcast_to(total, sums_send.shape)
    sums_all[me] = jnp.broadcast_to(total, sums_send.shape)

    own_row = jnp.concatenate([own_ref[0:1, :], own_ref[1:2, :]], axis=1)
    entries = own_row.shape[1]
    hits = own_row == lax.broadcasted_iota(jnp.int32, (n, entries), 0)
    earlier = lax.broadcasted_iota(jnp.int32, (entries, entries), 0) < lax.broadcasted_iota(
        jnp.int32, (entries, entries), 1
    )
    counts = mm(hits.astype(F32).astype(BF16), earlier.astype(F32).astype(BF16))
    rank = jnp.sum(jnp.where(hits, counts, 0.0), axis=0, keepdims=True)
    slot_row = own_row.astype(F32) * float(slots) + rank
    sea_row = sea_ref[...].astype(F32)
    slot0, slot1 = slot_row[:, :lon], slot_row[:, lon:]
    weight0 = wgt_ref[0:1, :] * sea_row
    weight1 = wgt_ref[1:2, :] * sea_row
    target = tgt_ref[...].astype(F32)
    target0 = jnp.broadcast_to(target[0:1, :], (8, lon)).astype(BF16)
    target1 = jnp.broadcast_to(target[1:2, :], (8, lon)).astype(BF16)

    def pack_one(p):
        place = (lax.broadcasted_iota(jnp.int32, (slots, lon), 0) + p * slots).astype(F32)
        hit0, hit1 = slot0 == place, slot1 == place
        pack[p] = (jnp.where(hit0, weight0, 0.0) + jnp.where(hit1, weight1, 0.0)).astype(BF16)
        cells_send[p] = mm_nt(target0, jnp.where(hit0, 1.0, 0.0).astype(BF16)) + mm_nt(
            target1, jnp.where(hit1, 1.0, 0.0).astype(BF16)
        )

    each(n, pack_one)
    cells_all[me] = cells_send[me]

    pl.semaphore_wait(barrier, n - 1)

    up = remote(atm_ref, north, halo_send.at[0], halo_recv.at[0], lax.rem(me + 1, n))
    down = remote(atm_ref, south, halo_send.at[1], halo_recv.at[1], lax.rem(me + n - 1, n))

    sum_copies, cell_copies = [], []
    for d in range(1, n):
        peer = lax.rem(me + d, n)
        sum_copies.append(
            remote(sums_send, sums_all.at[me], sum_send_sem.at[d], sum_recv_sem.at[d], peer)
        )
        sum_copies[-1].start()

    @pl.when(me < n - 1)
    def _():
        up.start()

    @pl.when(me > 0)
    def _():
        down.start()

    for d in range(1, n):
        peer = lax.rem(me + d, n)
        cell_copies.append(
            remote(
                cells_send.at[peer],
                cells_all.at[me],
                cell_send_sem.at[d],
                cell_recv_sem.at[d],
                peer,
            )
        )
        cell_copies[-1].start()

    @pl.when(me == 0)
    def _():
        north[...] = jnp.zeros_like(north)

    @pl.when(me == n - 1)
    def _():
        south[...] = jnp.zeros_like(south)

    stacked = jnp.concatenate(
        [slot0, slot1, weight0, weight1, jnp.zeros((4, lon), F32)], axis=0
    )
    columns = jnp.transpose(stacked)
    slot0c, slot1c = columns[:, 0:1], columns[:, 1:2]
    weight0c, weight1c = columns[:, 2:3], columns[:, 3:4]

    def unpack_one(p):
        place = (lax.broadcasted_iota(jnp.int32, (lon, slots), 1) + p * slots).astype(F32)
        unpack[:, pl.ds(p * slots, slots)] = (
            jnp.where(slot0c == place, weight0c, 0.0) + jnp.where(slot1c == place, weight1c, 0.0)
        ).astype(BF16)

    each(n, unpack_one)

    loads[0].wait()
    centre = atm_ref[...]
    taps = [mm(centre, conv_v[3 + b]) for b in range(3)]

    for copy in sum_copies:
        copy.wait_recv()
    zeros = jnp.zeros((8, channels), F32)

    def tally(p, sums):
        before, through, after = sums
        row = sums_all[p]
        before = before + jnp.where(p < me - 1, row, 0.0)
        through = through + jnp.where(p < me, row, 0.0)
        after = after + jnp.where((p >= 1) & (p <= me), row, 0.0)
        return before, through, after

    if n <= 8:
        carried = (zeros, zeros, zeros)
        for p in range(n):
            carried = tally(p, carried)
    else:
        carried = lax.fori_loop(0, n, tally, (zeros, zeros, zeros))
    mixed = jnp.zeros((8, channels), F32)
    for a in range(3):
        parts = thirds(carried[a])
        for b in range(3):
            mixed = mixed + mm(parts, conv_v[3 * a + b])
    prefix = (carried[1][0:1, :] + jnp.sum(mixed, axis=0, keepdims=True)) * (
        1.0 / (math.sqrt(lon) * math.sqrt(n))
    )
    loads[1].wait()
    meridional = jnp.sum(
        mm(thirds(jnp.broadcast_to(prefix, (8, channels))), mer_v[...]), axis=0, keepdims=True
    )

    for copy in cell_copies:
        copy.wait_recv()
    cells = ocn_v.shape[0]

    def gather_one(p):
        named = cells_all[p]
        rows = lax.broadcasted_iota(jnp.int32, (cells, slots), 0).astype(F32)
        gather_t[:, pl.ds(p * slots, slots)] = jnp.where(named[0:1, :] == rows, 1.0, 0.0).astype(
            BF16
        )
        lanes = lax.broadcasted_iota(jnp.int32, (slots, cells), 1).astype(F32)
        gather[p] = jnp.where(jnp.transpose(named)[:, 0:1] == lanes, 1.0, 0.0).astype(BF16)

    each(n, gather_one)

    for load in loads[2:]:
        load.wait()

    @pl.when(me > 0)
    def _():
        up.wait_recv()

    @pl.when(me < n - 1)
    def _():
        down.wait_recv()

    above, below = north[...], south[...]
    taps = [taps[b] + mm(above, conv_v[b]) + mm(below, conv_v[6 + b]) for b in range(3)]
    mixing = pltpu.roll(taps[0], 1, 0) + taps[1] + pltpu.roll(taps[2], lon - 1, 0)
    lifted = atm_ref[...].astype(F32) + mixing + meridional
    normed = rms_scale(lifted, again_ref[...]).astype(BF16)
    activated = silu(mm(normed, ain_v[...])).astype(BF16)
    atm_mid = (lifted + mm(activated, aout_v[...])).astype(BF16)
    mid_v[...] = atm_mid
    flux = mm(atm_mid, flux_v[...]).astype(BF16)

    flux_copies = []
    for d in range(1, n):
        peer = lax.rem(me + d, n)
        send_rows[peer] = mm(pack[peer], flux).astype(BF16)
        flux_copies.append(
            remote(
                send_rows.at[peer],
                recv_rows.at[me],
                flux_send_sem.at[d],
                flux_recv_sem.at[d],
                peer,
            )
        )
        flux_copies[-1].start()
    recv_rows[me] = mm(pack[me], flux).astype(BF16)
    for copy in flux_copies:
        copy.wait_recv()

    width = flux.shape[1]
    block = math.gcd(n, 8)

    def reduced(matrix, rows):
        def term(q, acc):
            part = rows[pl.ds(q * block, block)].reshape(block * slots, width)
            return acc + mm(matrix[:, pl.ds(q * block * slots, block * slots)], part)

        acc = jnp.zeros((matrix.shape[0], width), F32)
        if n == block:
            return term(0, acc)
        return lax.fori_loop(0, n // block, term, acc)

    forcing = reduced(gather_t, recv_rows).astype(BF16)
    ocean_lift = ocn_v[...].astype(F32) + mm(forcing, forc_v[...])
    ocean_normed = rms_scale(ocean_lift, ogain_ref[...]).astype(BF16)
    ocean_act = silu(mm(ocean_normed, oin_v[...])).astype(BF16)
    ocean_next = (ocean_lift + mm(ocean_act, oout_v[...])).astype(BF16)
    surface = mm(ocean_next, surf_v[...]).astype(BF16)

    back_copies = []
    for d in range(1, n):
        peer = lax.rem(me + d, n)
        back_rows[peer] = mm(gather[peer], surface).astype(BF16)
        back_copies.append(
            remote(
                back_rows.at[peer],
                ret_rows.at[me],
                back_send_sem.at[d],
                back_recv_sem.at[d],
                peer,
            )
        )
        back_copies[-1].start()
    ret_rows[me] = mm(gather[me], surface).astype(BF16)
    ocn_new[...] = ocean_next
    put = pltpu.make_async_copy(ocn_new, ocn_out_ref, out_sem)
    put.start()

    for copies in (sum_copies, cell_copies, flux_copies):
        for copy in copies:
            copy.wait_send()

    @pl.when(me < n - 1)
    def _():
        up.wait_send()

    @pl.when(me > 0)
    def _():
        down.wait_send()

    for copy in back_copies:
        copy.wait_recv()
    feedback = reduced(unpack, ret_rows).astype(BF16)
    atm_out_ref[...] = (mid_v[...].astype(F32) + mm(feedback, feed_v[...])).astype(BF16)
    for copy in back_copies:
        copy.wait_send()
    put.wait()


def local(
    atm_state,
    ocean_state,
    owners,
    target_cell,
    margin_weight,
    sea_mask,
    conv_kernel,
    meridional_weight,
    atm_gain,
    atm_in,
    atm_out,
    flux_weight,
    forcing_weight,
    ocean_gain,
    ocean_in,
    ocean_out,
    surface_weight,
    feedback_weight,
):
    _, lat_rows, lon, channels = atm_state.shape
    cells, ocn_ch = ocean_state.shape[1:]
    margins = owners.shape[-1]
    width = flux_weight.shape[1]
    n = lax.axis_size("space")
    assert lat_rows == 1 and margins == 2 and cells <= 256
    slots = max(2, 2 * lon * margins // n)
    slots = -(-slots // 128) * 128
    vmem = pl.BlockSpec(memory_space=pltpu.VMEM)
    hbm = pl.BlockSpec(memory_space=pl.ANY)
    weights = [
        ocean_state[0],
        conv_kernel,
        meridional_weight,
        atm_in,
        atm_out,
        flux_weight,
        forcing_weight,
        ocean_in,
        ocean_out,
        surface_weight,
        feedback_weight,
    ]
    dma = lambda count: pltpu.SemaphoreType.DMA((count,))
    atm_new, ocn_new = pl.pallas_call(
        functools.partial(kernel, n, slots),
        out_shape=(
            jax.ShapeDtypeStruct((lon, channels), BF16),
            jax.ShapeDtypeStruct((cells, ocn_ch), BF16),
        ),
        in_specs=[vmem] * 7 + [hbm] * len(weights),
        out_specs=(vmem, hbm),
        scratch_shapes=[pltpu.VMEM(w.shape, w.dtype) for w in weights]
        + [
            pltpu.VMEM((lon, channels), BF16),
            pltpu.VMEM((lon, channels), BF16),
            pltpu.VMEM((8, channels), F32),
            pltpu.VMEM((n, 8, channels), F32),
            pltpu.VMEM((n, 8, slots), F32),
            pltpu.VMEM((n, 8, slots), F32),
            pltpu.VMEM((n, slots, lon), BF16),
            pltpu.VMEM((lon, n * slots), BF16),
            pltpu.VMEM((cells, n * slots), BF16),
            pltpu.VMEM((n, slots, cells), BF16),
            pltpu.VMEM((n, slots, width), BF16),
            pltpu.VMEM((n, slots, width), BF16),
            pltpu.VMEM((n, slots, width), BF16),
            pltpu.VMEM((n, slots, width), BF16),
            pltpu.VMEM((lon, channels), BF16),
            pltpu.VMEM((cells, ocn_ch), BF16),
            dma(len(weights)),
            pltpu.SemaphoreType.DMA,
            dma(2),
            dma(2),
        ]
        + [dma(n)] * 8,
        compiler_params=pltpu.CompilerParams(
            collective_id=0, has_side_effects=True, vmem_limit_bytes=62 * 1024 * 1024
        ),
    )(
        atm_state.reshape(lon, channels),
        jnp.swapaxes(owners[0], 0, 1),
        jnp.swapaxes(target_cell[0], 0, 1),
        jnp.swapaxes(margin_weight[0], 0, 1),
        sea_mask,
        atm_gain[None, :],
        ocean_gain[None, :],
        *weights,
    )
    return atm_new.reshape(1, lat_rows, lon, channels), ocn_new[None]


def solution(mesh):
    state = P(("groups", "section"), "space", None, None)
    ocean = P(("groups", "section"), "space", None)
    margin = P("space", None, None)
    return jax.shard_map(
        local,
        mesh=mesh,
        in_specs=(state, ocean, margin, margin, margin, P("space", None)) + (P(),) * 12,
        out_specs=(state, ocean),
        check_vma=False,
    )
```

```python
import functools
import math

import jax
import jax.numpy as jnp
from jax import lax
from jax.experimental import pallas as pl
from jax.experimental.pallas import tpu as pltpu
from jax.sharding import PartitionSpec as P

F32 = jnp.float32
BF16 = jnp.bfloat16


def mm(left, right):
    return jnp.dot(left, right, preferred_element_type=F32)


def mm_nt(left, right):
    return lax.dot_general(left, right, (((1,), (1,)), ((), ())), preferred_element_type=F32)


def rms_scale(values, gain_vec):
    return values * lax.rsqrt(jnp.mean(values * values, axis=-1, keepdims=True) + 1e-06) * gain_vec


def silu(values):
    return values / (1.0 + jnp.exp(-values))


def thirds(rows):
    high = rows.astype(BF16).astype(F32)
    rest = rows - high
    middle = rest.astype(BF16).astype(F32)
    low = rest - middle
    row = lax.broadcasted_iota(jnp.int32, rows.shape, 0)
    return jnp.where(
        row == 0, high, jnp.where(row == 1, middle, jnp.where(row == 2, low, 0.0))
    ).astype(BF16)


def each(count, body):
    if count <= 8:
        for step in range(count):
            body(step)
    else:
        lax.fori_loop(0, count, lambda step, carry: (body(step), carry)[1], 0)


def kernel(
    n,
    slots,
    atm_ref,
    own_ref,
    tgt_ref,
    wgt_ref,
    sea_ref,
    again_ref,
    ogain_ref,
    conv_hbm,
    mer_hbm,
    ain_hbm,
    aout_hbm,
    flux_hbm,
    ocn_hbm,
    forc_hbm,
    oin_hbm,
    oout_hbm,
    surf_hbm,
    back_ref,
    mid_out_ref,
    ocn_out_ref,
    conv_v,
    mer_v,
    ain_v,
    aout_v,
    flux_v,
    ocn_v,
    forc_v,
    oin_v,
    oout_v,
    surf_v,
    north,
    south,
    sums_send,
    sums_all,
    cells_send,
    cells_all,
    pack,
    unpack,
    gather_t,
    gather,
    send_rows,
    recv_rows,
    back_rows,
    ret_rows,
    mid_v,
    ocn_new,
    load_sem,
    out_sem,
    halo_send,
    halo_recv,
    sum_send_sem,
    sum_recv_sem,
    cell_send_sem,
    cell_recv_sem,
    flux_send_sem,
    flux_recv_sem,
    back_send_sem,
    back_recv_sem,
):
    me = lax.axis_index("space")
    lon, channels = atm_ref.shape
    barrier = pltpu.get_barrier_semaphore()
    for d in range(1, n):
        pl.semaphore_signal(
            barrier,
            inc=1,
            device_id={"space": lax.rem(me + d, n)},
            device_id_type=pl.DeviceIdType.MESH,
        )

    loads = [
        pltpu.make_async_copy(src, dst, load_sem.at[i])
        for i, (src, dst) in enumerate(
            [
                (conv_hbm, conv_v),
                (mer_hbm, mer_v),
                (ain_hbm, ain_v),
                (aout_hbm, aout_v),
                (flux_hbm, flux_v),
                (ocn_hbm, ocn_v),
                (forc_hbm, forc_v),
                (oin_hbm, oin_v),
                (oout_hbm, oout_v),
                (surf_hbm, surf_v),
            ]
        )
    ]
    for load in loads:
        load.start()

    def remote(src, dst, send_sem, recv_sem, peer):
        return pltpu.make_async_remote_copy(
            src_ref=src,
            dst_ref=dst,
            send_sem=send_sem,
            recv_sem=recv_sem,
            device_id={"space": peer},
            device_id_type=pl.DeviceIdType.MESH,
        )

    total = jnp.sum(atm_ref[...].astype(F32), axis=0, keepdims=True)
    sums_send[...] = jnp.broadcast_to(total, sums_send.shape)
    sums_all[me] = jnp.broadcast_to(total, sums_send.shape)

    own_row = jnp.concatenate([own_ref[0:1, :], own_ref[1:2, :]], axis=1)
    entries = own_row.shape[1]
    hits = own_row == lax.broadcasted_iota(jnp.int32, (n, entries), 0)
    earlier = lax.broadcasted_iota(jnp.int32, (entries, entries), 0) < lax.broadcasted_iota(
        jnp.int32, (entries, entries), 1
    )
    counts = mm(hits.astype(F32).astype(BF16), earlier.astype(F32).astype(BF16))
    rank = jnp.sum(jnp.where(hits, counts, 0.0), axis=0, keepdims=True)
    slot_row = own_row.astype(F32) * float(slots) + rank
    sea_row = sea_ref[...].astype(F32)
    slot0, slot1 = slot_row[:, :lon], slot_row[:, lon:]
    weight0 = wgt_ref[0:1, :] * sea_row
    weight1 = wgt_ref[1:2, :] * sea_row
    target = tgt_ref[...].astype(F32)
    target0 = jnp.broadcast_to(target[0:1, :], (8, lon)).astype(BF16)
    target1 = jnp.broadcast_to(target[1:2, :], (8, lon)).astype(BF16)

    def pack_one(p):
        place = (lax.broadcasted_iota(jnp.int32, (slots, lon), 0) + p * slots).astype(F32)
        hit0, hit1 = slot0 == place, slot1 == place
        pack[p] = (jnp.where(hit0, weight0, 0.0) + jnp.where(hit1, weight1, 0.0)).astype(BF16)
        cells_send[p] = mm_nt(target0, jnp.where(hit0, 1.0, 0.0).astype(BF16)) + mm_nt(
            target1, jnp.where(hit1, 1.0, 0.0).astype(BF16)
        )

    each(n, pack_one)
    cells_all[me] = cells_send[me]

    pl.semaphore_wait(barrier, n - 1)

    up = remote(atm_ref, north, halo_send.at[0], halo_recv.at[0], lax.rem(me + 1, n))
    down = remote(atm_ref, south, halo_send.at[1], halo_recv.at[1], lax.rem(me + n - 1, n))

    sum_copies, cell_copies = [], []
    for d in range(1, n):
        peer = lax.rem(me + d, n)
        sum_copies.append(
            remote(sums_send, sums_all.at[me], sum_send_sem.at[d], sum_recv_sem.at[d], peer)
        )
        sum_copies[-1].start()

    @pl.when(me < n - 1)
    def _():
        up.start()

    @pl.when(me > 0)
    def _():
        down.start()

    for d in range(1, n):
        peer = lax.rem(me + d, n)
        cell_copies.append(
            remote(
                cells_send.at[peer],
                cells_all.at[me],
                cell_send_sem.at[d],
                cell_recv_sem.at[d],
                peer,
            )
        )
        cell_copies[-1].start()

    @pl.when(me == 0)
    def _():
        north[...] = jnp.zeros_like(north)

    @pl.when(me == n - 1)
    def _():
        south[...] = jnp.zeros_like(south)

    stacked = jnp.concatenate(
        [slot0, slot1, weight0, weight1, jnp.zeros((4, lon), F32)], axis=0
    )
    columns = jnp.transpose(stacked)
    slot0c, slot1c = columns[:, 0:1], columns[:, 1:2]
    weight0c, weight1c = columns[:, 2:3], columns[:, 3:4]

    def unpack_one(p):
        place = (lax.broadcasted_iota(jnp.int32, (lon, slots), 1) + p * slots).astype(F32)
        unpack[:, pl.ds(p * slots, slots)] = (
            jnp.where(slot0c == place, weight0c, 0.0) + jnp.where(slot1c == place, weight1c, 0.0)
        ).astype(BF16)

    each(n, unpack_one)

    loads[0].wait()
    centre = atm_ref[...]
    taps = [mm(centre, conv_v[3 + b]) for b in range(3)]

    for copy in sum_copies:
        copy.wait_recv()
    zeros = jnp.zeros((8, channels), F32)

    def tally(p, sums):
        before, through, after = sums
        row = sums_all[p]
        before = before + jnp.where(p < me - 1, row, 0.0)
        through = through + jnp.where(p < me, row, 0.0)
        after = after + jnp.where((p >= 1) & (p <= me), row, 0.0)
        return before, through, after

    if n <= 8:
        carried = (zeros, zeros, zeros)
        for p in range(n):
            carried = tally(p, carried)
    else:
        carried = lax.fori_loop(0, n, tally, (zeros, zeros, zeros))
    mixed = jnp.zeros((8, channels), F32)
    for a in range(3):
        parts = thirds(carried[a])
        for b in range(3):
            mixed = mixed + mm(parts, conv_v[3 * a + b])
    prefix = (carried[1][0:1, :] + jnp.sum(mixed, axis=0, keepdims=True)) * (
        1.0 / (math.sqrt(lon) * math.sqrt(n))
    )
    loads[1].wait()
    meridional = jnp.sum(
        mm(thirds(jnp.broadcast_to(prefix, (8, channels))), mer_v[...]), axis=0, keepdims=True
    )

    for copy in cell_copies:
        copy.wait_recv()
    cells = ocn_v.shape[1]

    def gather_one(p):
        named = cells_all[p]
        rows = lax.broadcasted_iota(jnp.int32, (cells, slots), 0).astype(F32)
        gather_t[:, pl.ds(p * slots, slots)] = jnp.where(named[0:1, :] == rows, 1.0, 0.0).astype(
            BF16
        )
        lanes = lax.broadcasted_iota(jnp.int32, (slots, cells), 1).astype(F32)
        gather[p] = jnp.where(jnp.transpose(named)[:, 0:1] == lanes, 1.0, 0.0).astype(BF16)

    each(n, gather_one)

    for load in loads[2:]:
        load.wait()

    @pl.when(me > 0)
    def _():
        up.wait_recv()

    @pl.when(me < n - 1)
    def _():
        down.wait_recv()

    above, below = north[...], south[...]
    taps = [taps[b] + mm(above, conv_v[b]) + mm(below, conv_v[6 + b]) for b in range(3)]
    mixing = pltpu.roll(taps[0], 1, 0) + taps[1] + pltpu.roll(taps[2], lon - 1, 0)
    lifted = atm_ref[...].astype(F32) + mixing + meridional
    normed = rms_scale(lifted, again_ref[...]).astype(BF16)
    activated = silu(mm(normed, ain_v[...])).astype(BF16)
    atm_mid = (lifted + mm(activated, aout_v[...])).astype(BF16)
    flux = mm(atm_mid, flux_v[...]).astype(BF16)

    flux_copies = []
    for d in range(1, n):
        peer = lax.rem(me + d, n)
        send_rows[peer] = mm(pack[peer], flux).astype(BF16)
        flux_copies.append(
            remote(
                send_rows.at[peer],
                recv_rows.at[me],
                flux_send_sem.at[d],
                flux_recv_sem.at[d],
                peer,
            )
        )
        flux_copies[-1].start()
    recv_rows[me] = mm(pack[me], flux).astype(BF16)
    mid_v[...] = atm_mid
    put_mid = pltpu.make_async_copy(mid_v, mid_out_ref, out_sem.at[0])
    put_mid.start()
    ocean = jnp.transpose(ocn_v[...].astype(F32))
    for copy in flux_copies:
        copy.wait_recv()

    width = flux.shape[1]
    block = math.gcd(n, 8)

    def reduced(matrix, rows):
        def term(q, acc):
            part = rows[pl.ds(q * block, block)].reshape(block * slots, width)
            return acc + mm(matrix[:, pl.ds(q * block * slots, block * slots)], part)

        acc = jnp.zeros((matrix.shape[0], width), F32)
        if n == block:
            return term(0, acc)
        return lax.fori_loop(0, n // block, term, acc)

    forcing = reduced(gather_t, recv_rows).astype(BF16)
    ocean_lift = ocean + mm_nt(forcing, forc_v[...])
    ocean_normed = rms_scale(ocean_lift, ogain_ref[...]).astype(BF16)
    ocean_act = silu(mm(ocean_normed, oin_v[...])).astype(BF16)
    ocean_new = ocean_lift + mm_nt(ocean_act, oout_v[...])
    ocean_next = ocean_new.astype(BF16)
    surface = mm(ocean_next, surf_v[...]).astype(BF16)

    back_copies = []
    for d in range(1, n):
        peer = lax.rem(me + d, n)
        back_rows[peer] = mm(gather[peer], surface).astype(BF16)
        back_copies.append(
            remote(
                back_rows.at[peer],
                ret_rows.at[me],
                back_send_sem.at[d],
                back_recv_sem.at[d],
                peer,
            )
        )
        back_copies[-1].start()
    ret_rows[me] = mm(gather[me], surface).astype(BF16)
    ocn_new[...] = jnp.transpose(ocean_new).astype(BF16)
    put_ocn = pltpu.make_async_copy(ocn_new, ocn_out_ref, out_sem.at[1])
    put_ocn.start()

    for copies in (sum_copies, cell_copies, flux_copies):
        for copy in copies:
            copy.wait_send()

    @pl.when(me < n - 1)
    def _():
        up.wait_send()

    @pl.when(me > 0)
    def _():
        down.wait_send()

    for copy in back_copies:
        copy.wait_recv()
    back_ref[...] = reduced(unpack, ret_rows).astype(BF16)
    for copy in back_copies:
        copy.wait_send()
    put_mid.wait()
    put_ocn.wait()


def finish(back_ref, mid_ref, ocn_ref, feed_ref, atm_out_ref, ocn_out_ref):
    ocn_out_ref[...] = ocn_ref[...]
    atm_out_ref[...] = (mid_ref[...].astype(F32) + mm(back_ref[...], feed_ref[...])).astype(BF16)


def local(
    atm_state,
    ocean_state,
    owners,
    target_cell,
    margin_weight,
    sea_mask,
    conv_kernel,
    meridional_weight,
    atm_gain,
    atm_in,
    atm_out,
    flux_weight,
    forcing_weight,
    ocean_gain,
    ocean_in,
    ocean_out,
    surface_weight,
    feedback_weight,
):
    _, lat_rows, lon, channels = atm_state.shape
    cells, ocn_ch = ocean_state.shape[1:]
    margins = owners.shape[-1]
    width = flux_weight.shape[1]
    n = lax.axis_size("space")
    assert lat_rows == 1 and margins == 2 and cells <= 256
    slots = max(2, 2 * lon * margins // n)
    slots = -(-slots // 128) * 128
    vmem = pl.BlockSpec(memory_space=pltpu.VMEM)
    hbm = pl.BlockSpec(memory_space=pl.ANY)
    weights = [
        conv_kernel,
        meridional_weight,
        atm_in,
        atm_out,
        flux_weight,
        jnp.swapaxes(ocean_state[0], 0, 1),
        jnp.swapaxes(forcing_weight, 0, 1),
        ocean_in,
        jnp.swapaxes(ocean_out, 0, 1),
        surface_weight,
    ]
    dma = lambda count: pltpu.SemaphoreType.DMA((count,))
    back, mid, ocn = pl.pallas_call(
        functools.partial(kernel, n, slots),
        out_shape=(
            jax.ShapeDtypeStruct((lon, width), BF16),
            jax.ShapeDtypeStruct((lon, channels), BF16),
            jax.ShapeDtypeStruct((ocn_ch, cells), BF16),
        ),
        in_specs=[vmem] * 7 + [hbm] * len(weights),
        out_specs=(vmem, hbm, hbm),
        scratch_shapes=[pltpu.VMEM(w.shape, w.dtype) for w in weights]
        + [
            pltpu.VMEM((lon, channels), BF16),
            pltpu.VMEM((lon, channels), BF16),
            pltpu.VMEM((8, channels), F32),
            pltpu.VMEM((n, 8, channels), F32),
            pltpu.VMEM((n, 8, slots), F32),
            pltpu.VMEM((n, 8, slots), F32),
            pltpu.VMEM((n, slots, lon), BF16),
            pltpu.VMEM((lon, n * slots), BF16),
            pltpu.VMEM((cells, n * slots), BF16),
            pltpu.VMEM((n, slots, cells), BF16),
            pltpu.VMEM((n, slots, width), BF16),
            pltpu.VMEM((n, slots, width), BF16),
            pltpu.VMEM((n, slots, width), BF16),
            pltpu.VMEM((n, slots, width), BF16),
            pltpu.VMEM((lon, channels), BF16),
            pltpu.VMEM((ocn_ch, cells), BF16),
            dma(len(weights)),
            dma(2),
            dma(2),
            dma(2),
        ]
        + [dma(n)] * 8,
        compiler_params=pltpu.CompilerParams(
            collective_id=0, has_side_effects=True, vmem_limit_bytes=62 * 1024 * 1024
        ),
    )(
        atm_state.reshape(lon, channels),
        jnp.swapaxes(owners[0], 0, 1),
        jnp.swapaxes(target_cell[0], 0, 1),
        jnp.swapaxes(margin_weight[0], 0, 1),
        sea_mask,
        atm_gain[None, :],
        ocean_gain[None, :],
        *weights,
    )
    atm_new, ocn_new = pl.pallas_call(
        finish,
        out_shape=(
            jax.ShapeDtypeStruct((lon, channels), BF16),
            jax.ShapeDtypeStruct((ocn_ch, cells), BF16),
        ),
        in_specs=[vmem] * 4,
        out_specs=(vmem, vmem),
    )(back, mid, ocn, feedback_weight)
    return atm_new.reshape(1, lat_rows, lon, channels), jnp.swapaxes(ocn_new, 0, 1)[None]


def solution(mesh):
    state = P(("groups", "section"), "space", None, None)
    ocean = P(("groups", "section"), "space", None)
    margin = P("space", None, None)
    return jax.shard_map(
        local,
        mesh=mesh,
        in_specs=(state, ocean, margin, margin, margin, P("space", None)) + (P(),) * 12,
        out_specs=(state, ocean),
        check_vma=False,
    )
```

```python
import functools
import math

import jax
import jax.numpy as jnp
from jax import lax
from jax.experimental import pallas as pl
from jax.experimental.pallas import tpu as pltpu
from jax.sharding import PartitionSpec as P

F32 = jnp.float32
BF16 = jnp.bfloat16


def mm(left, right):
    return jnp.dot(left, right, preferred_element_type=F32)


def mm_nt(left, right):
    return lax.dot_general(left, right, (((1,), (1,)), ((), ())), preferred_element_type=F32)


def rms_scale(values, gain_vec):
    return values * lax.rsqrt(jnp.mean(values * values, axis=-1, keepdims=True) + 1e-06) * gain_vec


def silu(values):
    return values / (1.0 + jnp.exp(-values))


def thirds(rows):
    high = rows.astype(BF16).astype(F32)
    rest = rows - high
    middle = rest.astype(BF16).astype(F32)
    low = rest - middle
    row = lax.broadcasted_iota(jnp.int32, rows.shape, 0)
    return jnp.where(
        row == 0, high, jnp.where(row == 1, middle, jnp.where(row == 2, low, 0.0))
    ).astype(BF16)


def each(count, body):
    if count <= 8:
        for step in range(count):
            body(step)
    else:
        lax.fori_loop(0, count, lambda step, carry: (body(step), carry)[1], 0)


def kernel(
    n,
    slots,
    atm_ref,
    own_ref,
    tgt_ref,
    wgt_ref,
    sea_ref,
    again_ref,
    ogain_ref,
    conv_hbm,
    mer_hbm,
    ain_hbm,
    aout_hbm,
    flux_hbm,
    ocn_hbm,
    forc_hbm,
    oin_hbm,
    oout_hbm,
    surf_hbm,
    back_ref,
    mid_out_ref,
    ocn_out_ref,
    conv_v,
    mer_v,
    ain_v,
    aout_v,
    flux_v,
    ocn_v,
    forc_v,
    oin_v,
    oout_v,
    surf_v,
    north,
    south,
    sums_send,
    sums_all,
    cells_send,
    cells_all,
    pack,
    unpack,
    gather_t,
    gather,
    send_rows,
    recv_rows,
    back_rows,
    ret_rows,
    mid_v,
    ocn_new,
    load_sem,
    out_sem,
    halo_send,
    halo_recv,
    sum_send_sem,
    sum_recv_sem,
    cell_send_sem,
    cell_recv_sem,
    flux_send_sem,
    flux_recv_sem,
    back_send_sem,
    back_recv_sem,
):
    me = lax.axis_index("space")
    lon, channels = atm_ref.shape
    barrier = pltpu.get_barrier_semaphore()
    for d in range(1, n):
        pl.semaphore_signal(
            barrier,
            inc=1,
            device_id={"space": lax.rem(me + d, n)},
            device_id_type=pl.DeviceIdType.MESH,
        )

    loads = [
        pltpu.make_async_copy(src, dst, load_sem.at[i])
        for i, (src, dst) in enumerate(
            [
                (conv_hbm, conv_v),
                (mer_hbm, mer_v),
                (ain_hbm, ain_v),
                (aout_hbm, aout_v),
                (flux_hbm, flux_v),
                (ocn_hbm, ocn_v),
                (forc_hbm, forc_v),
                (oin_hbm, oin_v),
                (oout_hbm, oout_v),
                (surf_hbm, surf_v),
            ]
        )
    ]
    for load in loads:
        load.start()

    def remote(src, dst, send_sem, recv_sem, peer):
        return pltpu.make_async_remote_copy(
            src_ref=src,
            dst_ref=dst,
            send_sem=send_sem,
            recv_sem=recv_sem,
            device_id={"space": peer},
            device_id_type=pl.DeviceIdType.MESH,
        )

    total = jnp.sum(atm_ref[...].astype(F32), axis=0, keepdims=True)
    sums_send[...] = jnp.broadcast_to(total, sums_send.shape)
    sums_all[me] = jnp.broadcast_to(total, sums_send.shape)

    pl.semaphore_wait(barrier, n - 1)

    sum_copies, cell_copies = [], []
    for d in range(1, n):
        peer = lax.rem(me + d, n)
        sum_copies.append(
            remote(sums_send, sums_all.at[me], sum_send_sem.at[d], sum_recv_sem.at[d], peer)
        )
        sum_copies[-1].start()

    up = remote(atm_ref, north, halo_send.at[0], halo_recv.at[0], lax.rem(me + 1, n))
    down = remote(atm_ref, south, halo_send.at[1], halo_recv.at[1], lax.rem(me + n - 1, n))

    @pl.when(me < n - 1)
    def _():
        up.start()

    @pl.when(me > 0)
    def _():
        down.start()

    @pl.when(me == 0)
    def _():
        north[...] = jnp.zeros_like(north)

    @pl.when(me == n - 1)
    def _():
        south[...] = jnp.zeros_like(south)

    own_row = jnp.concatenate([own_ref[0:1, :], own_ref[1:2, :]], axis=1)
    entries = own_row.shape[1]
    hits = own_row == lax.broadcasted_iota(jnp.int32, (n, entries), 0)
    earlier = lax.broadcasted_iota(jnp.int32, (entries, entries), 0) < lax.broadcasted_iota(
        jnp.int32, (entries, entries), 1
    )
    counts = mm(hits.astype(F32).astype(BF16), earlier.astype(F32).astype(BF16))
    rank = jnp.sum(jnp.where(hits, counts, 0.0), axis=0, keepdims=True)
    slot_row = own_row.astype(F32) * float(slots) + rank
    sea_row = sea_ref[...].astype(F32)
    slot0, slot1 = slot_row[:, :lon], slot_row[:, lon:]
    weight0 = wgt_ref[0:1, :] * sea_row
    weight1 = wgt_ref[1:2, :] * sea_row
    target = tgt_ref[...].astype(F32)
    target0 = jnp.broadcast_to(target[0:1, :], (8, lon)).astype(BF16)
    target1 = jnp.broadcast_to(target[1:2, :], (8, lon)).astype(BF16)

    def pack_one(p):
        place = (lax.broadcasted_iota(jnp.int32, (slots, lon), 0) + p * slots).astype(F32)
        hit0, hit1 = slot0 == place, slot1 == place
        pack[p] = (jnp.where(hit0, weight0, 0.0) + jnp.where(hit1, weight1, 0.0)).astype(BF16)
        cells_send[p] = mm_nt(target0, jnp.where(hit0, 1.0, 0.0).astype(BF16)) + mm_nt(
            target1, jnp.where(hit1, 1.0, 0.0).astype(BF16)
        )

    each(n, pack_one)
    cells_all[me] = cells_send[me]

    for d in range(1, n):
        peer = lax.rem(me + d, n)
        cell_copies.append(
            remote(
                cells_send.at[peer],
                cells_all.at[me],
                cell_send_sem.at[d],
                cell_recv_sem.at[d],
                peer,
            )
        )
        cell_copies[-1].start()

    loads[0].wait()
    centre = atm_ref[...]
    taps = [mm(centre, conv_v[3 + b]) for b in range(3)]

    for copy in sum_copies:
        copy.wait_recv()
    zeros = jnp.zeros((8, channels), F32)

    def tally(p, sums):
        before, through, after = sums
        row = sums_all[p]
        before = before + jnp.where(p < me - 1, row, 0.0)
        through = through + jnp.where(p < me, row, 0.0)
        after = after + jnp.where((p >= 1) & (p <= me), row, 0.0)
        return before, through, after

    if n <= 8:
        carried = (zeros, zeros, zeros)
        for p in range(n):
            carried = tally(p, carried)
    else:
        carried = lax.fori_loop(0, n, tally, (zeros, zeros, zeros))
    mixed = jnp.zeros((8, channels), F32)
    for a in range(3):
        parts = thirds(carried[a])
        for b in range(3):
            mixed = mixed + mm(parts, conv_v[3 * a + b])
    prefix = (carried[1][0:1, :] + jnp.sum(mixed, axis=0, keepdims=True)) * (
        1.0 / (math.sqrt(lon) * math.sqrt(n))
    )
    loads[1].wait()
    meridional = jnp.sum(
        mm(thirds(jnp.broadcast_to(prefix, (8, channels))), mer_v[...]), axis=0, keepdims=True
    )

    for load in loads[2:]:
        load.wait()

    @pl.when(me > 0)
    def _():
        up.wait_recv()

    @pl.when(me < n - 1)
    def _():
        down.wait_recv()

    above, below = north[...], south[...]
    taps = [taps[b] + mm(above, conv_v[b]) + mm(below, conv_v[6 + b]) for b in range(3)]
    mixing = pltpu.roll(taps[0], 1, 0) + taps[1] + pltpu.roll(taps[2], lon - 1, 0)
    lifted = atm_ref[...].astype(F32) + mixing + meridional
    normed = rms_scale(lifted, again_ref[...]).astype(BF16)
    activated = silu(mm(normed, ain_v[...])).astype(BF16)
    atm_mid = (lifted + mm(activated, aout_v[...])).astype(BF16)
    flux = mm(atm_mid, flux_v[...]).astype(BF16)

    flux_copies = []
    for d in range(1, n):
        peer = lax.rem(me + d, n)
        send_rows[peer] = mm(pack[peer], flux).astype(BF16)
        flux_copies.append(
            remote(
                send_rows.at[peer],
                recv_rows.at[me],
                flux_send_sem.at[d],
                flux_recv_sem.at[d],
                peer,
            )
        )
        flux_copies[-1].start()
    recv_rows[me] = mm(pack[me], flux).astype(BF16)
    mid_v[...] = atm_mid
    put_mid = pltpu.make_async_copy(mid_v, mid_out_ref, out_sem.at[0])
    put_mid.start()
    ocean = jnp.transpose(ocn_v[...].astype(F32))
    for copy in cell_copies:
        copy.wait_recv()
    cells = ocn_v.shape[1]

    def gather_one(p):
        named = cells_all[p]
        rows = lax.broadcasted_iota(jnp.int32, (cells, slots), 0).astype(F32)
        gather_t[:, pl.ds(p * slots, slots)] = jnp.where(named[0:1, :] == rows, 1.0, 0.0).astype(
            BF16
        )
        lanes = lax.broadcasted_iota(jnp.int32, (slots, cells), 1).astype(F32)
        gather[p] = jnp.where(jnp.transpose(named)[:, 0:1] == lanes, 1.0, 0.0).astype(BF16)

    each(n, gather_one)

    for copy in flux_copies:
        copy.wait_recv()

    width = flux.shape[1]
    block = math.gcd(n, 8)

    def reduced(matrix, rows):
        def term(q, acc):
            part = rows[pl.ds(q * block, block)].reshape(block * slots, width)
            return acc + mm(matrix[:, pl.ds(q * block * slots, block * slots)], part)

        acc = jnp.zeros((matrix.shape[0], width), F32)
        if n == block:
            return term(0, acc)
        return lax.fori_loop(0, n // block, term, acc)

    forcing = reduced(gather_t, recv_rows).astype(BF16)
    ocean_lift = ocean + mm_nt(forcing, forc_v[...])
    ocean_normed = rms_scale(ocean_lift, ogain_ref[...]).astype(BF16)
    ocean_act = silu(mm(ocean_normed, oin_v[...])).astype(BF16)
    ocean_new = ocean_lift + mm_nt(ocean_act, oout_v[...])
    ocean_next = ocean_new.astype(BF16)
    surface = mm(ocean_next, surf_v[...]).astype(BF16)

    back_copies = []
    for d in range(1, n):
        peer = lax.rem(me + d, n)
        back_rows[peer] = mm(gather[peer], surface).astype(BF16)
        back_copies.append(
            remote(
                back_rows.at[peer],
                ret_rows.at[me],
                back_send_sem.at[d],
                back_recv_sem.at[d],
                peer,
            )
        )
        back_copies[-1].start()
    ret_rows[me] = mm(gather[me], surface).astype(BF16)
    ocn_new[...] = jnp.transpose(ocean_new).astype(BF16)
    put_ocn = pltpu.make_async_copy(ocn_new, ocn_out_ref, out_sem.at[1])
    put_ocn.start()

    stacked = jnp.concatenate(
        [slot0, slot1, weight0, weight1, jnp.zeros((4, lon), F32)], axis=0
    )
    columns = jnp.transpose(stacked)
    slot0c, slot1c = columns[:, 0:1], columns[:, 1:2]
    weight0c, weight1c = columns[:, 2:3], columns[:, 3:4]

    def unpack_one(p):
        place = (lax.broadcasted_iota(jnp.int32, (lon, slots), 1) + p * slots).astype(F32)
        unpack[:, pl.ds(p * slots, slots)] = (
            jnp.where(slot0c == place, weight0c, 0.0) + jnp.where(slot1c == place, weight1c, 0.0)
        ).astype(BF16)

    each(n, unpack_one)

    for copies in (sum_copies, cell_copies, flux_copies):
        for copy in copies:
            copy.wait_send()

    @pl.when(me < n - 1)
    def _():
        up.wait_send()

    @pl.when(me > 0)
    def _():
        down.wait_send()

    for copy in back_copies:
        copy.wait_recv()
    back_ref[...] = reduced(unpack, ret_rows).astype(BF16)
    for copy in back_copies:
        copy.wait_send()
    put_mid.wait()
    put_ocn.wait()


def finish(back_ref, mid_ref, ocn_ref, feed_ref, atm_out_ref, ocn_out_ref):
    ocn_out_ref[...] = ocn_ref[...]
    atm_out_ref[...] = (mid_ref[...].astype(F32) + mm(back_ref[...], feed_ref[...])).astype(BF16)


def local(
    atm_state,
    ocean_state,
    owners,
    target_cell,
    margin_weight,
    sea_mask,
    conv_kernel,
    meridional_weight,
    atm_gain,
    atm_in,
    atm_out,
    flux_weight,
    forcing_weight,
    ocean_gain,
    ocean_in,
    ocean_out,
    surface_weight,
    feedback_weight,
):
    _, lat_rows, lon, channels = atm_state.shape
    cells, ocn_ch = ocean_state.shape[1:]
    margins = owners.shape[-1]
    width = flux_weight.shape[1]
    n = lax.axis_size("space")
    assert lat_rows == 1 and margins == 2 and cells <= 256
    slots = max(2, 2 * lon * margins // n)
    slots = -(-slots // 128) * 128
    vmem = pl.BlockSpec(memory_space=pltpu.VMEM)
    hbm = pl.BlockSpec(memory_space=pl.ANY)
    weights = [
        conv_kernel,
        meridional_weight,
        atm_in,
        atm_out,
        flux_weight,
        jnp.swapaxes(ocean_state[0], 0, 1),
        jnp.swapaxes(forcing_weight, 0, 1),
        ocean_in,
        jnp.swapaxes(ocean_out, 0, 1),
        surface_weight,
    ]
    dma = lambda count: pltpu.SemaphoreType.DMA((count,))
    back, mid, ocn = pl.pallas_call(
        functools.partial(kernel, n, slots),
        out_shape=(
            jax.ShapeDtypeStruct((lon, width), BF16),
            jax.ShapeDtypeStruct((lon, channels), BF16),
            jax.ShapeDtypeStruct((ocn_ch, cells), BF16),
        ),
        in_specs=[vmem] * 7 + [hbm] * len(weights),
        out_specs=(vmem, hbm, hbm),
        scratch_shapes=[pltpu.VMEM(w.shape, w.dtype) for w in weights]
        + [
            pltpu.VMEM((lon, channels), BF16),
            pltpu.VMEM((lon, channels), BF16),
            pltpu.VMEM((8, channels), F32),
            pltpu.VMEM((n, 8, channels), F32),
            pltpu.VMEM((n, 8, slots), F32),
            pltpu.VMEM((n, 8, slots), F32),
            pltpu.VMEM((n, slots, lon), BF16),
            pltpu.VMEM((lon, n * slots), BF16),
            pltpu.VMEM((cells, n * slots), BF16),
            pltpu.VMEM((n, slots, cells), BF16),
            pltpu.VMEM((n, slots, width), BF16),
            pltpu.VMEM((n, slots, width), BF16),
            pltpu.VMEM((n, slots, width), BF16),
            pltpu.VMEM((n, slots, width), BF16),
            pltpu.VMEM((lon, channels), BF16),
            pltpu.VMEM((ocn_ch, cells), BF16),
            dma(len(weights)),
            dma(2),
            dma(2),
            dma(2),
        ]
        + [dma(n)] * 8,
        compiler_params=pltpu.CompilerParams(
            collective_id=0, has_side_effects=True, vmem_limit_bytes=62 * 1024 * 1024
        ),
    )(
        atm_state.reshape(lon, channels),
        jnp.swapaxes(owners[0], 0, 1),
        jnp.swapaxes(target_cell[0], 0, 1),
        jnp.swapaxes(margin_weight[0], 0, 1),
        sea_mask,
        atm_gain[None, :],
        ocean_gain[None, :],
        *weights,
    )
    atm_new, ocn_new = pl.pallas_call(
        finish,
        out_shape=(
            jax.ShapeDtypeStruct((lon, channels), BF16),
            jax.ShapeDtypeStruct((ocn_ch, cells), BF16),
        ),
        in_specs=[vmem] * 4,
        out_specs=(vmem, vmem),
    )(back, mid, ocn, feedback_weight)
    return atm_new.reshape(1, lat_rows, lon, channels), jnp.swapaxes(ocn_new, 0, 1)[None]


def solution(mesh):
    state = P(("groups", "section"), "space", None, None)
    ocean = P(("groups", "section"), "space", None)
    margin = P("space", None, None)
    return jax.shard_map(
        local,
        mesh=mesh,
        in_specs=(state, ocean, margin, margin, margin, P("space", None)) + (P(),) * 12,
        out_specs=(state, ocean),
        check_vma=False,
    )
```

```python
import functools
import math

import jax
import jax.numpy as jnp
from jax import lax
from jax.experimental import pallas as pl
from jax.experimental.pallas import tpu as pltpu
from jax.sharding import PartitionSpec as P

F32 = jnp.float32
BF16 = jnp.bfloat16


def mm(left, right):
    return jnp.dot(left, right, preferred_element_type=F32)


def mm_nt(left, right):
    return lax.dot_general(left, right, (((1,), (1,)), ((), ())), preferred_element_type=F32)


def rms_scale(values, gain_vec):
    return values * lax.rsqrt(jnp.mean(values * values, axis=-1, keepdims=True) + 1e-06) * gain_vec


def silu(values):
    half = 0.5 * values
    return half + half * jnp.tanh(half)


def thirds(rows):
    high = rows.astype(BF16).astype(F32)
    rest = rows - high
    middle = rest.astype(BF16).astype(F32)
    low = rest - middle
    row = lax.broadcasted_iota(jnp.int32, rows.shape, 0)
    return jnp.where(
        row == 0, high, jnp.where(row == 1, middle, jnp.where(row == 2, low, 0.0))
    ).astype(BF16)


def each(count, body):
    if count <= 8:
        for step in range(count):
            body(step)
    else:
        lax.fori_loop(0, count, lambda step, carry: (body(step), carry)[1], 0)


def kernel(
    n,
    slots,
    atm_ref,
    own_ref,
    tgt_ref,
    wgt_ref,
    sea_ref,
    again_ref,
    ogain_ref,
    conv_hbm,
    mer_hbm,
    ain_hbm,
    aout_hbm,
    flux_hbm,
    ocn_hbm,
    forc_hbm,
    oin_hbm,
    oout_hbm,
    surf_hbm,
    back_ref,
    mid_out_ref,
    ocn_out_ref,
    conv_v,
    mer_v,
    ain_v,
    aout_v,
    flux_v,
    ocn_v,
    forc_v,
    oin_v,
    oout_v,
    surf_v,
    north,
    south,
    sums_send,
    sums_all,
    cells_send,
    cells_all,
    pack,
    unpack,
    gather_t,
    gather,
    send_rows,
    recv_rows,
    back_rows,
    ret_rows,
    mid_v,
    ocn_new,
    load_sem,
    out_sem,
    halo_send,
    halo_recv,
    sum_send_sem,
    sum_recv_sem,
    cell_send_sem,
    cell_recv_sem,
    flux_send_sem,
    flux_recv_sem,
    back_send_sem,
    back_recv_sem,
):
    me = lax.axis_index("space")
    lon, channels = atm_ref.shape
    barrier = pltpu.get_barrier_semaphore()
    for d in range(1, n):
        pl.semaphore_signal(
            barrier,
            inc=1,
            device_id={"space": lax.rem(me + d, n)},
            device_id_type=pl.DeviceIdType.MESH,
        )

    loads = [
        pltpu.make_async_copy(src, dst, load_sem.at[i])
        for i, (src, dst) in enumerate(
            [
                (conv_hbm, conv_v),
                (mer_hbm, mer_v),
                (ain_hbm, ain_v),
                (aout_hbm, aout_v),
                (flux_hbm, flux_v),
                (ocn_hbm, ocn_v),
                (forc_hbm, forc_v),
                (oin_hbm, oin_v),
                (oout_hbm, oout_v),
                (surf_hbm, surf_v),
            ]
        )
    ]
    for load in loads:
        load.start()

    def remote(src, dst, send_sem, recv_sem, peer):
        return pltpu.make_async_remote_copy(
            src_ref=src,
            dst_ref=dst,
            send_sem=send_sem,
            recv_sem=recv_sem,
            device_id={"space": peer},
            device_id_type=pl.DeviceIdType.MESH,
        )

    total = jnp.sum(atm_ref[...].astype(F32), axis=0, keepdims=True)
    sums_send[...] = total
    sums_all[me] = total

    pl.semaphore_wait(barrier, n - 1)

    sum_copies, cell_copies = [], []
    for d in range(1, n):
        peer = lax.rem(me + d, n)
        sum_copies.append(
            remote(sums_send, sums_all.at[me], sum_send_sem.at[d], sum_recv_sem.at[d], peer)
        )
        sum_copies[-1].start()

    up = remote(atm_ref, north, halo_send.at[0], halo_recv.at[0], lax.rem(me + 1, n))
    down = remote(atm_ref, south, halo_send.at[1], halo_recv.at[1], lax.rem(me + n - 1, n))

    @pl.when(me < n - 1)
    def _():
        up.start()

    @pl.when(me > 0)
    def _():
        down.start()

    @pl.when(me == 0)
    def _():
        north[...] = jnp.zeros_like(north)

    @pl.when(me == n - 1)
    def _():
        south[...] = jnp.zeros_like(south)

    own_row = jnp.concatenate([own_ref[0:1, :], own_ref[1:2, :]], axis=1)
    entries = own_row.shape[1]
    hits = own_row == lax.broadcasted_iota(jnp.int32, (n, entries), 0)
    earlier = lax.broadcasted_iota(jnp.int32, (entries, entries), 0) < lax.broadcasted_iota(
        jnp.int32, (entries, entries), 1
    )
    counts = mm(hits.astype(F32).astype(BF16), earlier.astype(F32).astype(BF16))
    rank = jnp.sum(jnp.where(hits, counts, 0.0), axis=0, keepdims=True)
    slot_row = own_row.astype(F32) * float(slots) + rank
    sea_row = sea_ref[...].astype(F32)
    slot0, slot1 = slot_row[:, :lon], slot_row[:, lon:]
    weight0 = wgt_ref[0:1, :] * sea_row
    weight1 = wgt_ref[1:2, :] * sea_row
    target = tgt_ref[...].astype(F32)
    target0 = jnp.broadcast_to(target[0:1, :], (8, lon)).astype(BF16)
    target1 = jnp.broadcast_to(target[1:2, :], (8, lon)).astype(BF16)

    def pack_one(p):
        place = (lax.broadcasted_iota(jnp.int32, (slots, lon), 0) + p * slots).astype(F32)
        hit0, hit1 = slot0 == place, slot1 == place
        pack[p] = (jnp.where(hit0, weight0, 0.0) + jnp.where(hit1, weight1, 0.0)).astype(BF16)
        named = mm_nt(target0, jnp.where(hit0, 1.0, 0.0).astype(BF16)) + mm_nt(
            target1, jnp.where(hit1, 1.0, 0.0).astype(BF16)
        )
        cells_send[p] = named[0:1, :]

    each(n, pack_one)
    cells_all[me] = cells_send[me]

    for d in range(1, n):
        peer = lax.rem(me + d, n)
        cell_copies.append(
            remote(
                cells_send.at[peer],
                cells_all.at[me],
                cell_send_sem.at[d],
                cell_recv_sem.at[d],
                peer,
            )
        )
        cell_copies[-1].start()

    loads[0].wait()
    centre = atm_ref[...]
    taps = [mm(centre, conv_v[3 + b]) for b in range(3)]

    for copy in sum_copies:
        copy.wait_recv()
    zeros = jnp.zeros((1, channels), F32)

    def tally(p, sums):
        before, through, after = sums
        row = sums_all[p]
        before = before + jnp.where(p < me - 1, row, 0.0)
        through = through + jnp.where(p < me, row, 0.0)
        after = after + jnp.where((p >= 1) & (p <= me), row, 0.0)
        return before, through, after

    if n <= 8:
        carried = (zeros, zeros, zeros)
        for p in range(n):
            carried = tally(p, carried)
    else:
        carried = lax.fori_loop(0, n, tally, (zeros, zeros, zeros))
    mixed = jnp.zeros((8, channels), F32)
    for a in range(3):
        parts = thirds(jnp.broadcast_to(carried[a], (8, channels)))
        for b in range(3):
            mixed = mixed + mm(parts, conv_v[3 * a + b])
    prefix = (carried[1] + jnp.sum(mixed, axis=0, keepdims=True)) * (
        1.0 / (math.sqrt(lon) * math.sqrt(n))
    )
    loads[1].wait()
    meridional = jnp.sum(
        mm(thirds(jnp.broadcast_to(prefix, (8, channels))), mer_v[...]), axis=0, keepdims=True
    )

    for load in loads[2:]:
        load.wait()

    @pl.when(me > 0)
    def _():
        up.wait_recv()

    @pl.when(me < n - 1)
    def _():
        down.wait_recv()

    above, below = north[...], south[...]
    taps = [taps[b] + mm(above, conv_v[b]) + mm(below, conv_v[6 + b]) for b in range(3)]
    mixing = pltpu.roll(taps[0], 1, 0) + taps[1] + pltpu.roll(taps[2], lon - 1, 0)
    lifted = atm_ref[...].astype(F32) + mixing + meridional
    normed = rms_scale(lifted, again_ref[...]).astype(BF16)
    activated = silu(mm(normed, ain_v[...])).astype(BF16)
    atm_mid = (lifted + mm(activated, aout_v[...])).astype(BF16)
    flux = mm(atm_mid, flux_v[...]).astype(BF16)

    flux_copies = []
    for d in range(1, n):
        peer = lax.rem(me + d, n)
        send_rows[peer] = mm(pack[peer], flux).astype(BF16)
        flux_copies.append(
            remote(
                send_rows.at[peer],
                recv_rows.at[me],
                flux_send_sem.at[d],
                flux_recv_sem.at[d],
                peer,
            )
        )
        flux_copies[-1].start()
    recv_rows[me] = mm(pack[me], flux).astype(BF16)
    mid_v[...] = atm_mid
    put_mid = pltpu.make_async_copy(mid_v, mid_out_ref, out_sem.at[0])
    put_mid.start()
    ocean = jnp.transpose(ocn_v[...].astype(F32))
    for copy in cell_copies:
        copy.wait_recv()
    cells = ocn_v.shape[1]

    def gather_one(p):
        named = jnp.broadcast_to(cells_all[p], (8, slots))
        rows = lax.broadcasted_iota(jnp.int32, (cells, slots), 0).astype(F32)
        gather_t[:, pl.ds(p * slots, slots)] = jnp.where(named[0:1, :] == rows, 1.0, 0.0).astype(
            BF16
        )
        lanes = lax.broadcasted_iota(jnp.int32, (slots, cells), 1).astype(F32)
        gather[p] = jnp.where(jnp.transpose(named)[:, 0:1] == lanes, 1.0, 0.0).astype(BF16)

    each(n, gather_one)

    for copy in flux_copies:
        copy.wait_recv()

    width = flux.shape[1]
    block = math.gcd(n, 8)

    def reduced(matrix, rows):
        def term(q, acc):
            part = rows[pl.ds(q * block, block)].reshape(block * slots, width)
            return acc + mm(matrix[:, pl.ds(q * block * slots, block * slots)], part)

        acc = jnp.zeros((matrix.shape[0], width), F32)
        if n == block:
            return term(0, acc)
        return lax.fori_loop(0, n // block, term, acc)

    forcing = reduced(gather_t, recv_rows).astype(BF16)
    ocean_lift = ocean + mm_nt(forcing, forc_v[...])
    ocean_normed = rms_scale(ocean_lift, ogain_ref[...]).astype(BF16)
    ocean_act = silu(mm(ocean_normed, oin_v[...])).astype(BF16)
    ocean_new = ocean_lift + mm_nt(ocean_act, oout_v[...])
    ocean_next = ocean_new.astype(BF16)
    surface = mm(ocean_next, surf_v[...]).astype(BF16)

    back_copies = []
    for d in range(1, n):
        peer = lax.rem(me + d, n)
        back_rows[peer] = mm(gather[peer], surface).astype(BF16)
        back_copies.append(
            remote(
                back_rows.at[peer],
                ret_rows.at[me],
                back_send_sem.at[d],
                back_recv_sem.at[d],
                peer,
            )
        )
        back_copies[-1].start()
    ret_rows[me] = mm(gather[me], surface).astype(BF16)
    ocn_new[...] = jnp.transpose(ocean_new).astype(BF16)
    put_ocn = pltpu.make_async_copy(ocn_new, ocn_out_ref, out_sem.at[1])
    put_ocn.start()

    stacked = jnp.concatenate(
        [slot0, slot1, weight0, weight1, jnp.zeros((4, lon), F32)], axis=0
    )
    columns = jnp.transpose(stacked)
    slot0c, slot1c = columns[:, 0:1], columns[:, 1:2]
    weight0c, weight1c = columns[:, 2:3], columns[:, 3:4]

    def unpack_one(p):
        place = (lax.broadcasted_iota(jnp.int32, (lon, slots), 1) + p * slots).astype(F32)
        unpack[:, pl.ds(p * slots, slots)] = (
            jnp.where(slot0c == place, weight0c, 0.0) + jnp.where(slot1c == place, weight1c, 0.0)
        ).astype(BF16)

    each(n, unpack_one)

    for copies in (sum_copies, cell_copies, flux_copies):
        for copy in copies:
            copy.wait_send()

    @pl.when(me < n - 1)
    def _():
        up.wait_send()

    @pl.when(me > 0)
    def _():
        down.wait_send()

    for copy in back_copies:
        copy.wait_recv()
    back_ref[...] = reduced(unpack, ret_rows).astype(BF16)
    for copy in back_copies:
        copy.wait_send()
    put_mid.wait()
    put_ocn.wait()


def finish(back_ref, mid_ref, ocn_ref, feed_ref, atm_out_ref, ocn_out_ref):
    ocn_out_ref[...] = ocn_ref[...]
    atm_out_ref[...] = (mid_ref[...].astype(F32) + mm(back_ref[...], feed_ref[...])).astype(BF16)


def local(
    atm_state,
    ocean_state,
    owners,
    target_cell,
    margin_weight,
    sea_mask,
    conv_kernel,
    meridional_weight,
    atm_gain,
    atm_in,
    atm_out,
    flux_weight,
    forcing_weight,
    ocean_gain,
    ocean_in,
    ocean_out,
    surface_weight,
    feedback_weight,
):
    _, lat_rows, lon, channels = atm_state.shape
    cells, ocn_ch = ocean_state.shape[1:]
    margins = owners.shape[-1]
    width = flux_weight.shape[1]
    n = lax.axis_size("space")
    assert lat_rows == 1 and margins == 2 and cells <= 256
    slots = max(2, 2 * lon * margins // n)
    slots = -(-slots // 128) * 128
    vmem = pl.BlockSpec(memory_space=pltpu.VMEM)
    hbm = pl.BlockSpec(memory_space=pl.ANY)
    weights = [
        conv_kernel,
        meridional_weight,
        atm_in,
        atm_out,
        flux_weight,
        jnp.swapaxes(ocean_state[0], 0, 1),
        jnp.swapaxes(forcing_weight, 0, 1),
        ocean_in,
        jnp.swapaxes(ocean_out, 0, 1),
        surface_weight,
    ]
    dma = lambda count: pltpu.SemaphoreType.DMA((count,))
    back, mid, ocn = pl.pallas_call(
        functools.partial(kernel, n, slots),
        out_shape=(
            jax.ShapeDtypeStruct((lon, width), BF16),
            jax.ShapeDtypeStruct((lon, channels), BF16),
            jax.ShapeDtypeStruct((ocn_ch, cells), BF16),
        ),
        in_specs=[vmem] * 7 + [hbm] * len(weights),
        out_specs=(vmem, hbm, hbm),
        scratch_shapes=[pltpu.VMEM(w.shape, w.dtype) for w in weights]
        + [
            pltpu.VMEM((lon, channels), BF16),
            pltpu.VMEM((lon, channels), BF16),
            pltpu.VMEM((1, channels), F32),
            pltpu.VMEM((n, 1, channels), F32),
            pltpu.VMEM((n, 1, slots), F32),
            pltpu.VMEM((n, 1, slots), F32),
            pltpu.VMEM((n, slots, lon), BF16),
            pltpu.VMEM((lon, n * slots), BF16),
            pltpu.VMEM((cells, n * slots), BF16),
            pltpu.VMEM((n, slots, cells), BF16),
            pltpu.VMEM((n, slots, width), BF16),
            pltpu.VMEM((n, slots, width), BF16),
            pltpu.VMEM((n, slots, width), BF16),
            pltpu.VMEM((n, slots, width), BF16),
            pltpu.VMEM((lon, channels), BF16),
            pltpu.VMEM((ocn_ch, cells), BF16),
            dma(len(weights)),
            dma(2),
            dma(2),
            dma(2),
        ]
        + [dma(n)] * 8,
        compiler_params=pltpu.CompilerParams(
            collective_id=0, has_side_effects=True, vmem_limit_bytes=62 * 1024 * 1024
        ),
    )(
        atm_state.reshape(lon, channels),
        jnp.swapaxes(owners[0], 0, 1),
        jnp.swapaxes(target_cell[0], 0, 1),
        jnp.swapaxes(margin_weight[0], 0, 1),
        sea_mask,
        atm_gain[None, :],
        ocean_gain[None, :],
        *weights,
    )
    atm_new, ocn_new = pl.pallas_call(
        finish,
        out_shape=(
            jax.ShapeDtypeStruct((lon, channels), BF16),
            jax.ShapeDtypeStruct((ocn_ch, cells), BF16),
        ),
        in_specs=[vmem] * 4,
        out_specs=(vmem, vmem),
    )(back, mid, ocn, feedback_weight)
    return atm_new.reshape(1, lat_rows, lon, channels), jnp.swapaxes(ocn_new, 0, 1)[None]


def solution(mesh):
    state = P(("groups", "section"), "space", None, None)
    ocean = P(("groups", "section"), "space", None)
    margin = P("space", None, None)
    return jax.shard_map(
        local,
        mesh=mesh,
        in_specs=(state, ocean, margin, margin, margin, P("space", None)) + (P(),) * 12,
        out_specs=(state, ocean),
        check_vma=False,
    )
```

```python
import functools
import math

import jax
import jax.numpy as jnp
from jax import lax
from jax.experimental import pallas as pl
from jax.experimental.pallas import tpu as pltpu
from jax.sharding import PartitionSpec as P

F32 = jnp.float32
BF16 = jnp.bfloat16


def mm(left, right):
    return jnp.dot(left, right, preferred_element_type=F32)


def mm_nt(left, right):
    return lax.dot_general(left, right, (((1,), (1,)), ((), ())), preferred_element_type=F32)


def rms_scale(values, gain_vec):
    return values * lax.rsqrt(jnp.mean(values * values, axis=-1, keepdims=True) + 1e-06) * gain_vec


def silu(values):
    half = 0.5 * values
    return half + half * jnp.tanh(half)


def thirds(rows):
    high = rows.astype(BF16).astype(F32)
    rest = rows - high
    middle = rest.astype(BF16).astype(F32)
    low = rest - middle
    row = lax.broadcasted_iota(jnp.int32, rows.shape, 0)
    return jnp.where(
        row == 0, high, jnp.where(row == 1, middle, jnp.where(row == 2, low, 0.0))
    ).astype(BF16)


def each(count, body):
    if count <= 8:
        for step in range(count):
            body(step)
    else:
        lax.fori_loop(0, count, lambda step, carry: (body(step), carry)[1], 0)


def kernel(
    n,
    slots,
    atm_ref,
    own_ref,
    tgt_ref,
    wgt_ref,
    sea_ref,
    again_ref,
    ogain_ref,
    conv_hbm,
    mer_hbm,
    ain_hbm,
    aout_hbm,
    flux_hbm,
    ocn_hbm,
    forc_hbm,
    oin_hbm,
    oout_hbm,
    surf_hbm,
    back_ref,
    mid_out_ref,
    ocn_out_ref,
    conv_v,
    mer_v,
    ain_v,
    aout_v,
    flux_v,
    ocn_v,
    forc_v,
    oin_v,
    oout_v,
    surf_v,
    north,
    south,
    sums_send,
    sums_all,
    cells_send,
    cells_all,
    pack,
    unpack,
    gather_t,
    gather,
    send_rows,
    recv_rows,
    back_rows,
    ret_rows,
    mid_v,
    ocn_new,
    load_sem,
    out_sem,
    halo_send,
    halo_recv,
    sum_send_sem,
    sum_recv_sem,
    cell_send_sem,
    cell_recv_sem,
    flux_send_sem,
    flux_recv_sem,
    back_send_sem,
    back_recv_sem,
):
    me = lax.axis_index("space")
    lon, channels = atm_ref.shape
    barrier = pltpu.get_barrier_semaphore()
    for d in range(1, n):
        pl.semaphore_signal(
            barrier,
            inc=1,
            device_id={"space": lax.rem(me + d, n)},
            device_id_type=pl.DeviceIdType.MESH,
        )

    loads = [
        pltpu.make_async_copy(src, dst, load_sem.at[i])
        for i, (src, dst) in enumerate(
            [
                (conv_hbm, conv_v),
                (mer_hbm, mer_v),
                (ain_hbm, ain_v),
                (aout_hbm, aout_v),
                (flux_hbm, flux_v),
                (ocn_hbm, ocn_v),
                (forc_hbm, forc_v),
                (oin_hbm, oin_v),
                (oout_hbm, oout_v),
                (surf_hbm, surf_v),
            ]
        )
    ]
    for load in loads:
        load.start()

    def remote(src, dst, send_sem, recv_sem, peer):
        return pltpu.make_async_remote_copy(
            src_ref=src,
            dst_ref=dst,
            send_sem=send_sem,
            recv_sem=recv_sem,
            device_id={"space": peer},
            device_id_type=pl.DeviceIdType.MESH,
        )

    total = jnp.sum(atm_ref[...].astype(F32), axis=0, keepdims=True)
    sums_send[...] = total
    sums_all[me] = total

    pl.semaphore_wait(barrier, n - 1)

    sum_copies, cell_copies = [], []
    for d in range(1, n):
        peer = lax.rem(me + d, n)
        sum_copies.append(
            remote(sums_send, sums_all.at[me], sum_send_sem.at[d], sum_recv_sem.at[d], peer)
        )
        sum_copies[-1].start()

    up = remote(atm_ref, north, halo_send.at[0], halo_recv.at[0], lax.rem(me + 1, n))
    down = remote(atm_ref, south, halo_send.at[1], halo_recv.at[1], lax.rem(me + n - 1, n))

    @pl.when(me < n - 1)
    def _():
        up.start()

    @pl.when(me > 0)
    def _():
        down.start()

    @pl.when(me == 0)
    def _():
        north[...] = jnp.zeros_like(north)

    @pl.when(me == n - 1)
    def _():
        south[...] = jnp.zeros_like(south)

    own_row = jnp.concatenate([own_ref[0:1, :], own_ref[1:2, :]], axis=1)
    entries = own_row.shape[1]
    hits = own_row == lax.broadcasted_iota(jnp.int32, (n, entries), 0)
    earlier = lax.broadcasted_iota(jnp.int32, (entries, entries), 0) < lax.broadcasted_iota(
        jnp.int32, (entries, entries), 1
    )
    counts = mm(hits.astype(F32).astype(BF16), earlier.astype(F32).astype(BF16))
    rank = jnp.sum(jnp.where(hits, counts, 0.0), axis=0, keepdims=True)
    slot_row = own_row.astype(F32) * float(slots) + rank
    sea_row = sea_ref[...].astype(F32)
    slot0, slot1 = slot_row[:, :lon], slot_row[:, lon:]
    weight0 = wgt_ref[0:1, :] * sea_row
    weight1 = wgt_ref[1:2, :] * sea_row
    target = tgt_ref[...].astype(F32)
    target0 = jnp.broadcast_to(target[0:1, :], (8, lon)).astype(BF16)
    target1 = jnp.broadcast_to(target[1:2, :], (8, lon)).astype(BF16)

    def pack_one(p):
        place = (lax.broadcasted_iota(jnp.int32, (slots, lon), 0) + p * slots).astype(F32)
        hit0, hit1 = slot0 == place, slot1 == place
        pack[p] = (jnp.where(hit0, weight0, 0.0) + jnp.where(hit1, weight1, 0.0)).astype(BF16)
        named = mm_nt(target0, jnp.where(hit0, 1.0, 0.0).astype(BF16)) + mm_nt(
            target1, jnp.where(hit1, 1.0, 0.0).astype(BF16)
        )
        cells_send[p] = named[0:1, :]

    each(n, pack_one)
    cells_all[me] = cells_send[me]

    for d in range(1, n):
        peer = lax.rem(me + d, n)
        cell_copies.append(
            remote(
                cells_send.at[peer],
                cells_all.at[me],
                cell_send_sem.at[d],
                cell_recv_sem.at[d],
                peer,
            )
        )
        cell_copies[-1].start()

    loads[0].wait()
    centre = atm_ref[...]
    taps = [mm(centre, conv_v[3 + b]) for b in range(3)]

    for copy in sum_copies:
        copy.wait_recv()
    zeros = jnp.zeros((1, channels), F32)

    def tally(p, sums):
        before, through, after = sums
        row = sums_all[p]
        before = before + jnp.where(p < me - 1, row, 0.0)
        through = through + jnp.where(p < me, row, 0.0)
        after = after + jnp.where((p >= 1) & (p <= me), row, 0.0)
        return before, through, after

    if n <= 8:
        carried = (zeros, zeros, zeros)
        for p in range(n):
            carried = tally(p, carried)
    else:
        carried = lax.fori_loop(0, n, tally, (zeros, zeros, zeros))
    mixed = jnp.zeros((8, channels), F32)
    for a in range(3):
        parts = thirds(jnp.broadcast_to(carried[a], (8, channels)))
        for b in range(3):
            mixed = mixed + mm(parts, conv_v[3 * a + b])
    prefix = (carried[1] + jnp.sum(mixed, axis=0, keepdims=True)) * (
        1.0 / (math.sqrt(lon) * math.sqrt(n))
    )
    loads[1].wait()
    meridional = jnp.sum(
        mm(thirds(jnp.broadcast_to(prefix, (8, channels))), mer_v[...]), axis=0, keepdims=True
    )

    for load in loads[2:]:
        load.wait()

    @pl.when(me > 0)
    def _():
        up.wait_recv()

    above = north[...]
    taps = [taps[b] + mm(above, conv_v[b]) for b in range(3)]

    @pl.when(me < n - 1)
    def _():
        down.wait_recv()

    below = south[...]
    taps = [taps[b] + mm(below, conv_v[6 + b]) for b in range(3)]
    mixing = pltpu.roll(taps[0], 1, 0) + taps[1] + pltpu.roll(taps[2], lon - 1, 0)
    lifted = atm_ref[...].astype(F32) + mixing + meridional
    normed = rms_scale(lifted, again_ref[...]).astype(BF16)
    activated = silu(mm(normed, ain_v[...])).astype(BF16)
    atm_mid = (lifted + mm(activated, aout_v[...])).astype(BF16)
    flux = mm(atm_mid, flux_v[...]).astype(BF16)

    flux_copies = []
    for d in range(1, n):
        peer = lax.rem(me + d, n)
        send_rows[peer] = mm(pack[peer], flux).astype(BF16)
        flux_copies.append(
            remote(
                send_rows.at[peer],
                recv_rows.at[me],
                flux_send_sem.at[d],
                flux_recv_sem.at[d],
                peer,
            )
        )
        flux_copies[-1].start()
    recv_rows[me] = mm(pack[me], flux).astype(BF16)
    mid_v[...] = atm_mid
    put_mid = pltpu.make_async_copy(mid_v, mid_out_ref, out_sem.at[0])
    put_mid.start()
    ocean = jnp.transpose(ocn_v[...].astype(F32))
    for copy in cell_copies:
        copy.wait_recv()
    cells = ocn_v.shape[1]

    def gather_one(p):
        named = jnp.broadcast_to(cells_all[p], (8, slots))
        rows = lax.broadcasted_iota(jnp.int32, (cells, slots), 0).astype(F32)
        gather_t[:, pl.ds(p * slots, slots)] = jnp.where(named[0:1, :] == rows, 1.0, 0.0).astype(
            BF16
        )
        lanes = lax.broadcasted_iota(jnp.int32, (slots, cells), 1).astype(F32)
        gather[p] = jnp.where(jnp.transpose(named)[:, 0:1] == lanes, 1.0, 0.0).astype(BF16)

    each(n, gather_one)

    width = flux.shape[1]

    def reduced(matrix, rows, copies):
        acc = jnp.zeros((matrix.shape[0], width), F32)
        for d in range(n):
            if d > 0:
                copies[d - 1].wait_recv()
            source = lax.rem(me + n - d, n)
            lanes = pl.ds(pl.multiple_of(source * slots, 128), slots)
            acc = acc + mm(matrix[:, lanes], rows[source])
        return acc

    forcing = reduced(gather_t, recv_rows, flux_copies).astype(BF16)
    ocean_lift = ocean + mm_nt(forcing, forc_v[...])
    ocean_normed = rms_scale(ocean_lift, ogain_ref[...]).astype(BF16)
    ocean_act = silu(mm(ocean_normed, oin_v[...])).astype(BF16)
    ocean_new = ocean_lift + mm_nt(ocean_act, oout_v[...])
    ocean_next = ocean_new.astype(BF16)
    surface = mm(ocean_next, surf_v[...]).astype(BF16)

    back_copies = []
    for d in range(1, n):
        peer = lax.rem(me + d, n)
        back_rows[peer] = mm(gather[peer], surface).astype(BF16)
        back_copies.append(
            remote(
                back_rows.at[peer],
                ret_rows.at[me],
                back_send_sem.at[d],
                back_recv_sem.at[d],
                peer,
            )
        )
        back_copies[-1].start()
    ret_rows[me] = mm(gather[me], surface).astype(BF16)
    ocn_new[...] = jnp.transpose(ocean_new).astype(BF16)
    put_ocn = pltpu.make_async_copy(ocn_new, ocn_out_ref, out_sem.at[1])
    put_ocn.start()

    stacked = jnp.concatenate(
        [slot0, slot1, weight0, weight1, jnp.zeros((4, lon), F32)], axis=0
    )
    columns = jnp.transpose(stacked)
    slot0c, slot1c = columns[:, 0:1], columns[:, 1:2]
    weight0c, weight1c = columns[:, 2:3], columns[:, 3:4]

    def unpack_one(p):
        place = (lax.broadcasted_iota(jnp.int32, (lon, slots), 1) + p * slots).astype(F32)
        unpack[:, pl.ds(p * slots, slots)] = (
            jnp.where(slot0c == place, weight0c, 0.0) + jnp.where(slot1c == place, weight1c, 0.0)
        ).astype(BF16)

    each(n, unpack_one)

    for copies in (sum_copies, cell_copies, flux_copies):
        for copy in copies:
            copy.wait_send()

    @pl.when(me < n - 1)
    def _():
        up.wait_send()

    @pl.when(me > 0)
    def _():
        down.wait_send()

    back_ref[...] = reduced(unpack, ret_rows, back_copies).astype(BF16)
    for copy in back_copies:
        copy.wait_send()
    put_mid.wait()
    put_ocn.wait()


def finish(back_ref, mid_ref, ocn_ref, feed_ref, atm_out_ref, ocn_out_ref):
    ocn_out_ref[...] = ocn_ref[...]
    atm_out_ref[...] = (mid_ref[...].astype(F32) + mm(back_ref[...], feed_ref[...])).astype(BF16)


def local(
    atm_state,
    ocean_state,
    owners,
    target_cell,
    margin_weight,
    sea_mask,
    conv_kernel,
    meridional_weight,
    atm_gain,
    atm_in,
    atm_out,
    flux_weight,
    forcing_weight,
    ocean_gain,
    ocean_in,
    ocean_out,
    surface_weight,
    feedback_weight,
):
    _, lat_rows, lon, channels = atm_state.shape
    cells, ocn_ch = ocean_state.shape[1:]
    margins = owners.shape[-1]
    width = flux_weight.shape[1]
    n = lax.axis_size("space")
    assert lat_rows == 1 and margins == 2 and cells <= 256
    slots = max(2, 2 * lon * margins // n)
    slots = -(-slots // 128) * 128
    vmem = pl.BlockSpec(memory_space=pltpu.VMEM)
    hbm = pl.BlockSpec(memory_space=pl.ANY)
    weights = [
        conv_kernel,
        meridional_weight,
        atm_in,
        atm_out,
        flux_weight,
        jnp.swapaxes(ocean_state[0], 0, 1),
        jnp.swapaxes(forcing_weight, 0, 1),
        ocean_in,
        jnp.swapaxes(ocean_out, 0, 1),
        surface_weight,
    ]
    dma = lambda count: pltpu.SemaphoreType.DMA((count,))
    back, mid, ocn = pl.pallas_call(
        functools.partial(kernel, n, slots),
        out_shape=(
            jax.ShapeDtypeStruct((lon, width), BF16),
            jax.ShapeDtypeStruct((lon, channels), BF16),
            jax.ShapeDtypeStruct((ocn_ch, cells), BF16),
        ),
        in_specs=[vmem] * 7 + [hbm] * len(weights),
        out_specs=(vmem, hbm, hbm),
        scratch_shapes=[pltpu.VMEM(w.shape, w.dtype) for w in weights]
        + [
            pltpu.VMEM((lon, channels), BF16),
            pltpu.VMEM((lon, channels), BF16),
            pltpu.VMEM((1, channels), F32),
            pltpu.VMEM((n, 1, channels), F32),
            pltpu.VMEM((n, 1, slots), F32),
            pltpu.VMEM((n, 1, slots), F32),
            pltpu.VMEM((n, slots, lon), BF16),
            pltpu.VMEM((lon, n * slots), BF16),
            pltpu.VMEM((cells, n * slots), BF16),
            pltpu.VMEM((n, slots, cells), BF16),
            pltpu.VMEM((n, slots, width), BF16),
            pltpu.VMEM((n, slots, width), BF16),
            pltpu.VMEM((n, slots, width), BF16),
            pltpu.VMEM((n, slots, width), BF16),
            pltpu.VMEM((lon, channels), BF16),
            pltpu.VMEM((ocn_ch, cells), BF16),
            dma(len(weights)),
            dma(2),
            dma(2),
            dma(2),
        ]
        + [dma(n)] * 8,
        compiler_params=pltpu.CompilerParams(
            collective_id=0, has_side_effects=True, vmem_limit_bytes=62 * 1024 * 1024
        ),
    )(
        atm_state.reshape(lon, channels),
        jnp.swapaxes(owners[0], 0, 1),
        jnp.swapaxes(target_cell[0], 0, 1),
        jnp.swapaxes(margin_weight[0], 0, 1),
        sea_mask,
        atm_gain[None, :],
        ocean_gain[None, :],
        *weights,
    )
    atm_new, ocn_new = pl.pallas_call(
        finish,
        out_shape=(
            jax.ShapeDtypeStruct((lon, channels), BF16),
            jax.ShapeDtypeStruct((ocn_ch, cells), BF16),
        ),
        in_specs=[vmem] * 4,
        out_specs=(vmem, vmem),
    )(back, mid, ocn, feedback_weight)
    return atm_new.reshape(1, lat_rows, lon, channels), jnp.swapaxes(ocn_new, 0, 1)[None]


def solution(mesh):
    state = P(("groups", "section"), "space", None, None)
    ocean = P(("groups", "section"), "space", None)
    margin = P("space", None, None)
    return jax.shard_map(
        local,
        mesh=mesh,
        in_specs=(state, ocean, margin, margin, margin, P("space", None)) + (P(),) * 12,
        out_specs=(state, ocean),
        check_vma=False,
    )
```
